256 devices in a mesh: row: 16 (over y, z_hi, core), col: 16 (over x, z_lo).
Axes of the slice: x: 4, y: 4, z: 8 (z_hi: 2, z_lo: 4; z = z_hi * 4 + z_lo), core: 2. Of those that a mesh axis runs over, the one named last changes fastest.
Arguments:
- inputs: bfloat16 [512, 8192], P(None, 'row'), may hold values from -6 to 6
- out_grad: bfloat16 [512, 8192], P(None, 'row'), may hold values from -6 to 6
- gate_weight: bfloat16 [8192, 28672], P('row', 'col'), may hold values from -0.125 to 0.125
- up_weight: bfloat16 [8192, 28672], P('row', 'col'), may hold values from -0.125 to 0.125
- down_weight: bfloat16 [28672, 8192], P('col', 'row'), may hold values from -0.0625 to 0.0625
- gate_mask: int32 [64, 224], P('row', 'col'), may hold values from 0 to 1, as said below
- up_mask: int32 [64, 224], P('row', 'col'), may hold values from 0 to 1, as said below
- down_mask: int32 [224, 64], P('col', 'row'), may hold values from 0 to 1, as said below
Outputs:
- input_grad: bfloat16 [512, 8192], P('col', 'row')
- gate_grad: bfloat16 [8192, 28672], P('row', 'col')
- up_grad: bfloat16 [8192, 28672], P('row', 'col')
- down_grad: bfloat16 [28672, 8192], P('col', 'row')
The draws below stay inside these ranges and needn't reach their ends.
Inputs may be any that keep to these rules, and one draw needn't show every extreme that they name: `gate_mask`: 1 marks a kept 128 x 128 block of the gate projection; the share kept varies over row and column blocks. `up_mask`: 1 marks a kept 128 x 128 block of the up projection; the share kept varies over row and column blocks. `down_mask`: 1 marks a kept 128 x 128 block of the down projection; the share kept varies over row and column blocks.
All inputs are finite; a program needn't handle non-finite values.
Results may differ from the reference program's by a relative error of at most 0.0049.
Values may be sent and summed in bfloat16 or wider, within the bound.
A program may use at most 128 MiB of HBM per device.

```python
import jax
import jax.numpy as jnp
from jax import lax

D = 8192
FF = 28672
BLOCK = 128
TOKENS = 512
N_ROW = 16
N_COL = 16


def band_mask(key, row_blocks, col_blocks):
    key_rows, key_cols, key_pick = jax.random.split(key, 3)
    row_level = jax.random.randint(key_rows, (row_blocks, 1), 50, 300)
    col_level = jax.random.randint(key_cols, (1, col_blocks), 50, 300)
    rolled = jax.random.randint(key_pick, (row_blocks, col_blocks), 0, 1000)
    return (rolled < row_level + col_level).astype(jnp.int32)


def draw_gate_mask(key, part):
    return band_mask(jax.random.fold_in(key, 11), D // BLOCK, FF // BLOCK)


def draw_up_mask(key, part):
    return band_mask(jax.random.fold_in(key, 23), D // BLOCK, FF // BLOCK)


def draw_down_mask(key, part):
    return band_mask(jax.random.fold_in(key, 37), FF // BLOCK, D // BLOCK)


def shard_levels(rng, dims, pieces, least, high):
    def one(dim, shards_of):
        heights = jax.random.uniform(jax.random.fold_in(jax.random.fold_in(rng, 6), dim), (shards_of,), jnp.float32, least / len(pieces), high / len(pieces))
        return jnp.repeat(jnp.exp(heights), dims[dim] // shards_of).reshape((-1,) + (1,) * (len(dims) - dim - 1))

    level = one(*pieces[0])
    for cut in pieces[1:]:
        level = level * one(*cut)
    return level


def centred(own_key, shape, scale, most, cuts=(), kind=jnp.bfloat16):
    values = scale * jax.random.normal(own_key, shape, jnp.float32)
    if cuts:
        values = values * shard_levels(own_key, shape, cuts, -0.22, 0.18)
    return jnp.clip(values, -most, most).astype(kind)


def setup_inputs(seed: int = 0) -> dict:
    key_of = jax.random.split(jax.random.key(seed), 9)
    inputs = centred(key_of[0], (TOKENS, D), 1.0, 6.0, ((1, 16),))
    out_grad = centred(key_of[1], (TOKENS, D), 1.0, 6.0, ((1, 16),))
    gate_weight = centred(key_of[2], (D, FF), (3 * D // 10) ** -0.5, 0.125, ((0, 16), (1, 16)))
    up_weight = centred(key_of[3], (D, FF), (3 * D // 10) ** -0.5, 0.125, ((0, 16), (1, 16)))
    down_weight = centred(key_of[4], (FF, D), (3 * FF // 10) ** -0.5, 0.0625, ((0, 16), (1, 16)))
    gate_mask = draw_gate_mask(jax.random.fold_in(key_of[8], 71), 0)
    up_mask = draw_up_mask(jax.random.fold_in(key_of[8], 71), 0)
    down_mask = draw_down_mask(jax.random.fold_in(key_of[8], 71), 0)
    return {"inputs": inputs, "out_grad": out_grad, "gate_weight": gate_weight, "up_weight": up_weight, "down_weight": down_weight, "gate_mask": gate_mask, "up_mask": up_mask, "down_mask": down_mask}


def spread(values, keep_mask):
    row_blocks, col_blocks = keep_mask.shape
    row_size = values.shape[0] // row_blocks
    col_size = values.shape[1] // col_blocks
    shaped = values.reshape(row_blocks, row_size, col_blocks, col_size)
    return (shaped * keep_mask.astype(values.dtype)[:, None, :, None]).reshape(values.shape)


def grouped_sum(pairs, groups):
    left, right, left_dim, right_dim = pairs[0]
    width = left.shape[left_dim] // groups
    out_rows = left.shape[1 - left_dim]
    out_cols = right.shape[1 - right_dim]

    def add_group(index, total):
        start = index.astype(jnp.int32) * jnp.int32(width)
        term = jnp.zeros((out_rows, out_cols), jnp.float32)
        for former, latter, former_dim, latter_dim in pairs:
            former_part = lax.dynamic_slice_in_dim(former, start, width, former_dim)
            latter_part = lax.dynamic_slice_in_dim(latter, start, width, latter_dim)
            term = term + lax.dot_general(former_part, latter_part, (((former_dim,), (latter_dim,)), ((), ())), preferred_element_type=jnp.float32)
        return total + term

    return lax.fori_loop(0, groups, add_group, jnp.zeros((out_rows, out_cols), jnp.float32))


def masked_product(former, latter, keep_mask):
    panel_count = N_COL
    width = latter.shape[1] // panel_count
    latter_panels = latter.reshape(latter.shape[0], panel_count, width).transpose(1, 0, 2)
    mask_panels = keep_mask.reshape(keep_mask.shape[0], panel_count, keep_mask.shape[1] // panel_count).transpose(1, 0, 2)

    def one_panel(operands):
        product = jnp.dot(former.T, operands[0], preferred_element_type=jnp.float32)
        return spread(product, operands[1]).astype(jnp.bfloat16)

    stacked = lax.map(one_panel, (latter_panels, mask_panels))
    return stacked.transpose(1, 0, 2).reshape(former.shape[1], latter.shape[1])


def reference(inputs, out_grad, gate_weight, up_weight, down_weight, gate_mask, up_mask, down_mask):
    gate_full = spread(gate_weight, gate_mask)
    up_full = spread(up_weight, up_mask)
    down_full = spread(down_weight, down_mask)
    gate_sum = grouped_sum([(inputs, gate_full, 1, 0)], N_ROW)
    up_sum = grouped_sum([(inputs, up_full, 1, 0)], N_ROW)
    back_sum = grouped_sum([(out_grad, down_full, 1, 1)], N_ROW)
    sigmoid_gate = jax.nn.sigmoid(gate_sum)
    hidden = (gate_sum * sigmoid_gate * up_sum).astype(jnp.bfloat16)
    slope = sigmoid_gate * (1.0 + gate_sum * (1.0 - sigmoid_gate))
    gate_delta = (back_sum * up_sum * slope).astype(jnp.bfloat16)
    up_delta = (back_sum * gate_sum * sigmoid_gate).astype(jnp.bfloat16)
    input_grad = grouped_sum([(gate_delta, gate_full, 1, 1), (up_delta, up_full, 1, 1)], N_COL).astype(jnp.bfloat16)
    gate_grad = masked_product(inputs, gate_delta, gate_mask)
    up_grad = masked_product(inputs, up_delta, up_mask)
    down_grad = masked_product(hidden, out_grad, down_mask)
    return (input_grad, gate_grad, up_grad, down_grad)
```

```python
import jax
import jax.numpy as jnp
from jax import lax
from jax.experimental import pallas as pl
from jax.experimental.pallas import tpu as pltpu
from jax.sharding import PartitionSpec as P

MESH = pl.DeviceIdType.MESH
F32 = jnp.float32
BF16 = jnp.bfloat16
BLOCK = 128
TOK = 512
DIM = 512
FF = 1792
HALF = FF // 2
CHUNKS = 4
ROWS = 16
STEPS = 3 * CHUNKS

LAG_FORWARD = 2
LAG_OWN = 4
LAG_FINAL = 7
LAG_SPREAD = 10
LAG_RELAY = 12
LAG_CORE = 14
LAG_GRAD = 15

R1, R2, R3, L1, L2, L3 = range(6)


def product(left, right):
    return jnp.dot(left, right, preferred_element_type=F32)


def product_t(left, right):
    return lax.dot_general(left, right, (((1,), (1,)), ((), ())), preferred_element_type=F32)


def t_product(left, right):
    return lax.dot_general(left, right, (((0,), (0,)), ((), ())), preferred_element_type=F32)


def exchange_kernel(
    x_hbm, og_hbm, wg_hbm, wu_hbm, wd_hbm, gm, um, dm,
    d_hbm, ig_out,
    x_own, og_own, x_oth, og_oth, w_own, wd_own, w_oth, wd_oth,
    part, send, ring, z_out, z_in, halves, final, deltas,
    ig, ig_send, ig_ring, ig_sum, ig_in,
    local_sem, core_s, core_r, ring_s, ring_r, z_s, z_r, ag_s, ag_r, x_s, x_r, zl_s, zl_r,
):
    row = lax.axis_index("row")
    col = lax.axis_index("col")
    y = row // 4
    h = (row // 2) % 2
    c = row % 2
    x = col // 4
    zl = col % 4
    up = lax.rem(y + 1, 4)
    down = lax.rem(y + 3, 4)
    far = lax.rem(y + 2, 4)
    right = (up * 4 + h * 2 + c, col)
    left = (down * 4 + h * 2 + c, col)
    z_dev = (y * 4 + (1 - h) * 2 + c, col)
    core_dev = (y * 4 + h * 2 + (1 - c), col)
    x_right = (row, lax.rem(x + 1, 4) * 4 + zl)
    x_left = (row, lax.rem(x + 3, 4) * 4 + zl)
    own_cols = pl.ds(pl.multiple_of(c * HALF, 128), HALF)
    oth_cols = pl.ds(pl.multiple_of((1 - c) * HALF, 128), HALF)

    def remote(src, dst, ss, rs, dev):
        return pltpu.make_async_remote_copy(
            src_ref=src, dst_ref=dst, send_sem=ss, recv_sem=rs, device_id=dev, device_id_type=MESH
        )

    def piece(yy, hh):
        return pl.ds(pl.multiple_of(yy * 32 + hh * ROWS, ROWS), ROWS)

    loads = [
        pltpu.make_async_copy(wg_hbm, w_own.at[0], local_sem.at[0]),
        pltpu.make_async_copy(x_hbm, x_own, local_sem.at[1]),
        pltpu.make_async_copy(wu_hbm, w_own.at[1], local_sem.at[2]),
        pltpu.make_async_copy(wd_hbm, wd_own, local_sem.at[3]),
        pltpu.make_async_copy(og_hbm, og_own, local_sem.at[4]),
    ]
    for load in loads:
        load.start()

    bar = pltpu.get_barrier_semaphore()
    friends = [right, left, z_dev, core_dev, x_right, x_left]
    friends += [(row, x * 4 + lax.rem(zl + d, 4)) for d in (1, 2, 3)]
    for dev in friends:
        pl.semaphore_signal(bar, inc=1, device_id=dev, device_id_type=MESH)
    pl.semaphore_wait(bar, len(friends))

    core_sends = [
        remote(x_hbm, x_oth, core_s.at[0], core_r.at[0], core_dev),
        remote(w_own.at[0, :, oth_cols], w_oth.at[0], core_s.at[1], core_r.at[1], core_dev),
        remote(w_own.at[1, :, oth_cols], w_oth.at[1], core_s.at[2], core_r.at[2], core_dev),
        remote(og_hbm, og_oth, core_s.at[3], core_r.at[3], core_dev),
        remote(wd_own.at[pl.ds(pl.multiple_of((1 - c) * HALF, 128), HALF)], wd_oth, core_s.at[4], core_r.at[4], core_dev),
    ]
    core_sends[0].start()

    def mask_cols(which, mask_ref):
        @pl.loop(0, FF // BLOCK)
        def _(j):
            cols = pl.ds(pl.multiple_of(j * BLOCK, BLOCK), BLOCK)
            for i in range(DIM // BLOCK):
                rows = pl.ds(i * BLOCK, BLOCK)
                keep = jnp.full((BLOCK, BLOCK), mask_ref[i, j].astype(F32), F32).astype(BF16)
                w_own[which, rows, cols] = w_own[which, rows, cols] * keep

    def mask_rows():
        @pl.loop(0, FF // BLOCK)
        def _(j):
            rows = pl.ds(pl.multiple_of(j * BLOCK, BLOCK), BLOCK)
            for i in range(DIM // BLOCK):
                cols = pl.ds(i * BLOCK, BLOCK)
                keep = jnp.full((BLOCK, BLOCK), dm[j, i].astype(F32), F32).astype(BF16)
                wd_own[rows, cols] = wd_own[rows, cols] * keep

    loads[0].wait()
    mask_cols(0, gm)
    core_sends[1].start()
    loads[2].wait()
    mask_cols(1, um)
    core_sends[2].start()
    core_sends[3].start()
    loads[3].wait()
    mask_rows()
    core_sends[4].start()
    loads[1].wait()
    loads[4].wait()

    def ring_copy(kind, s, yy, hh):
        dev = right if kind in (R1, R2, R3) else left
        return remote(send.at[s, piece(yy, hh)], ring.at[kind, s], ring_s.at[kind, s], ring_r.at[kind, s], dev)

    def ring_pieces(s):
        return [
            ring_copy(R1, s, far, 0),
            ring_copy(L1, s, far, 1),
            ring_copy(R2, s, up, 1),
            ring_copy(L2, s, down, 0),
            ring_copy(R3, s, up, 0),
            ring_copy(L3, s, down, 1),
        ]

    def z_copy(s):
        return remote(z_out.at[s], z_in.at[s], z_s.at[s], z_r.at[s], z_dev)

    def ag_copy(t, k, yy, hh, dev):
        ref = deltas.at[pl.ds(1, 2), t, piece(yy, hh), own_cols]
        return remote(ref, ref, ag_s.at[t, k], ag_r.at[t, k], dev)

    def ag_core(t):
        ref = deltas.at[pl.ds(1, 2), t, :, own_cols]
        return remote(ref, ref, ag_s.at[t, 7], ag_r.at[t, 7], core_dev)

    def ag_core_in(t):
        ref = deltas.at[pl.ds(1, 2), t, :, oth_cols]
        return remote(ref, ref, ag_s.at[t, 7], ag_r.at[t, 7], core_dev)

    def h_copy(k, yy, hh, dev):
        ref = deltas.at[0, :, piece(yy, hh), own_cols]
        return remote(ref, ref, ag_s.at[CHUNKS, k], ag_r.at[CHUNKS, k], dev)

    def gather_own(copy):
        copy(0, y, h, z_dev).start()
        copy(1 + h, y, h, right).start()
        copy(3 + h, y, h, left).start()

    def gather_partner(copy):
        copy(0, y, 1 - h, z_dev).wait_recv()
        copy(2 - h, y, 1 - h, right).start()
        copy(4 - h, y, 1 - h, left).start()

    def gather_relay(copy):
        copy(1, down, 0, right).wait_recv()
        copy(5, down, 0, right).start()
        copy(4, up, 1, left).wait_recv()
        copy(6, up, 1, left).start()

    def gather_rest(copy):
        copy(2, down, 1, right).wait_recv()
        copy(3, up, 0, left).wait_recv()
        copy(5, far, 0, right).wait_recv()
        copy(6, far, 1, left).wait_recv()

    def gather_drain(copy):
        copy(0, y, h, z_dev).wait_send()
        for hh in range(2):
            copy(1 + hh, y, hh, right).wait_send()
            copy(3 + hh, y, hh, left).wait_send()
        copy(5, down, 0, right).wait_send()
        copy(6, up, 1, left).wait_send()

    def out_copy(t):
        return pltpu.make_async_copy(deltas.at[pl.ds(1, 2), t], d_hbm.at[pl.ds(1, 2), t], local_sem.at[5 + t])

    def at_chunk(s, lag, fn):
        @pl.when((s >= lag + 2) & (s < STEPS + lag) & (lax.rem(s + 3 * 16 - lag, 3) == 2))
        def _():
            fn((s - lag) // 3)

    @pl.loop(0, STEPS + LAG_GRAD)
    def _(s):
        @pl.when(s < STEPS)
        def _():
            m = lax.rem(s, 3)
            t = s // 3
            rows = pl.ds(pl.multiple_of(t * 128, 128), 128)

            @pl.when(s == 0)
            def _():
                core_sends[0].wait_recv()
                core_sends[1].wait_recv()

            @pl.when(s == 1)
            def _():
                core_sends[2].wait_recv()

            @pl.when(s == 2)
            def _():
                core_sends[3].wait_recv()
                core_sends[4].wait_recv()

            @pl.when(m < 2)
            def _():
                p = product(x_own[rows, :], w_own[m, :, own_cols]) + product(x_oth[rows, :], w_oth[m])
                part[s] = p
                send[s] = p.astype(BF16)

            @pl.when(m == 2)
            def _():
                mine = wd_own[own_cols, :]
                p = product_t(og_own[rows, :], mine) + product_t(og_oth[rows, :], wd_oth[...])
                part[s] = p
                send[s] = p.astype(BF16)

            for copy in ring_pieces(s)[:4]:
                copy.start()

        @pl.when((s >= LAG_FORWARD) & (s < STEPS + LAG_FORWARD))
        def _():
            n = s - LAG_FORWARD
            copies = ring_pieces(n)
            copies[0].wait_recv()
            send[n, piece(up, 0)] = (part[n, piece(up, 0)] + ring[R1, n].astype(F32)).astype(BF16)
            copies[4].start()
            copies[1].wait_recv()
            send[n, piece(down, 1)] = (part[n, piece(down, 1)] + ring[L1, n].astype(F32)).astype(BF16)
            copies[5].start()

        @pl.when((s >= LAG_OWN) & (s < STEPS + LAG_OWN))
        def _():
            n = s - LAG_OWN
            copies = ring_pieces(n)
            for copy in copies[2:]:
                copy.wait_recv()
            halves[n, 0] = part[n, piece(y, 0)] + ring[R3, n].astype(F32) + ring[L2, n].astype(F32)
            halves[n, 1] = part[n, piece(y, 1)] + ring[L3, n].astype(F32) + ring[R2, n].astype(F32)
            z_out[n] = halves[n, 1 - h].astype(BF16)
            z_copy(n).start()

        @pl.when((s >= LAG_FINAL) & (s < STEPS + LAG_FINAL))
        def _():
            n = s - LAG_FINAL
            z_copy(n).wait_recv()
            final[n] = halves[n, h] + z_in[n].astype(F32)

        def pointwise(t):
            gate = final[3 * t]
            upv = final[3 * t + 1]
            back = final[3 * t + 2]
            sig = jax.nn.sigmoid(gate)
            mine = piece(y, h)
            deltas[0, t, mine, own_cols] = (gate * sig * upv).astype(BF16)
            slope = sig * (1.0 + gate * (1.0 - sig))
            deltas[1, t, mine, own_cols] = (back * upv * slope).astype(BF16)
            deltas[2, t, mine, own_cols] = (back * gate * sig).astype(BF16)
            gather_own(lambda *a: ag_copy(t, *a))

            @pl.when(t == CHUNKS - 1)
            def _():
                h_copy(0, y, h, z_dev).start()

        def spread_partner(t):
            gather_partner(lambda *a: ag_copy(t, *a))

            @pl.when(t == CHUNKS - 1)
            def _():
                h_copy(1 + h, y, h, right).start()
                h_copy(3 + h, y, h, left).start()

        def relay(t):
            gather_relay(lambda *a: ag_copy(t, *a))

            @pl.when(t == CHUNKS - 1)
            def _():
                gather_partner(h_copy)

        def to_core(t):
            gather_rest(lambda *a: ag_copy(t, *a))
            ag_core(t).start()

        def grad(t):
            ag_core_in(t).wait_recv()
            out_copy(t).start()
            value = product_t(deltas[1, t], w_own[0]) + product_t(deltas[2, t], w_own[1])
            ig[t] = value
            ig_send[t] = value.astype(BF16)

        at_chunk(s, LAG_FINAL, pointwise)
        at_chunk(s, LAG_SPREAD, spread_partner)
        at_chunk(s, LAG_RELAY, relay)
        at_chunk(s, LAG_CORE, to_core)
        at_chunk(s, LAG_GRAD, grad)

    x_up = lax.rem(x + 1, 4)
    x_down = lax.rem(x + 3, 4)
    x_far = lax.rem(x + 2, 4)

    def x_copy(kind, q, half):
        dev = x_right if kind in (R1, R2, R3) else x_left
        return remote(ig_send.at[q, pl.ds(half * 64, 64)], ig_ring.at[kind], x_s.at[kind], x_r.at[kind], dev)

    x_copies = [
        x_copy(R1, x_far, 0),
        x_copy(L1, x_far, 1),
        x_copy(R2, x_up, 1),
        x_copy(L2, x_down, 0),
        x_copy(R3, x_up, 0),
        x_copy(L3, x_down, 1),
    ]
    for copy in x_copies[:4]:
        copy.start()
    gather_relay(h_copy)
    x_copies[0].wait_recv()
    ig_send[x_up, pl.ds(0, 64)] = (ig[x_up, pl.ds(0, 64)] + ig_ring[R1].astype(F32)).astype(BF16)
    x_copies[4].start()
    x_copies[1].wait_recv()
    ig_send[x_down, pl.ds(64, 64)] = (ig[x_down, pl.ds(64, 64)] + ig_ring[L1].astype(F32)).astype(BF16)
    x_copies[5].start()
    for copy in x_copies[2:]:
        copy.wait_recv()
    ig_sum[pl.ds(0, 64)] = ig[x, pl.ds(0, 64)] + ig_ring[R3].astype(F32) + ig_ring[L2].astype(F32)
    ig_sum[pl.ds(64, 64)] = ig[x, pl.ds(64, 64)] + ig_ring[L3].astype(F32) + ig_ring[R2].astype(F32)

    def zl_copy(d):
        to = lax.rem(zl + d, 4)
        return remote(
            ig_sum.at[pl.ds(pl.multiple_of(to * 32, 32), 32)], ig_in.at[d - 1], zl_s.at[d - 1], zl_r.at[d - 1], (row, x * 4 + to)
        )

    for d in (2, 3, 1):
        zl_copy(d).start()

    gather_rest(h_copy)
    h_ref = deltas.at[0, :, :, own_cols]
    h_core = remote(h_ref, h_ref, ag_s.at[CHUNKS, 7], ag_r.at[CHUNKS, 7], core_dev)
    h_core.start()

    total = ig_sum[pl.ds(pl.multiple_of(zl * 32, 32), 32)]
    for d in (1, 2, 3):
        zl_copy(d).wait_recv()
        total = total + ig_in[d - 1]
    ig_out[...] = total.astype(BF16)

    h_in = deltas.at[0, :, :, oth_cols]
    remote(h_in, h_in, ag_s.at[CHUNKS, 7], ag_r.at[CHUNKS, 7], core_dev).wait_recv()
    h_store = pltpu.make_async_copy(deltas.at[0], d_hbm.at[0], local_sem.at[5 + CHUNKS])
    h_store.start()

    for copy in core_sends:
        copy.wait_send()

    @pl.loop(0, STEPS)
    def _(s):
        for copy in ring_pieces(s):
            copy.wait_send()
        z_copy(s).wait_send()

    @pl.loop(0, CHUNKS)
    def _(t):
        gather_drain(lambda *a: ag_copy(t, *a))
        ag_core(t).wait_send()
        out_copy(t).wait()

    gather_drain(h_copy)
    h_core.wait_send()
    for copy in x_copies:
        copy.wait_send()
    for d in (1, 2, 3):
        zl_copy(d).wait_send()
    h_store.wait()


def exchange(inputs, out_grad, gate_weight, up_weight, down_weight, gate_mask, up_mask, down_mask):
    any_spec = pl.BlockSpec(memory_space=pl.ANY)
    smem = pl.BlockSpec(memory_space=pltpu.SMEM)
    dma = pltpu.SemaphoreType.DMA
    return pl.pallas_call(
        exchange_kernel,
        out_shape=(
            jax.ShapeDtypeStruct((3, CHUNKS, 128, FF), BF16),
            jax.ShapeDtypeStruct((32, DIM), BF16),
        ),
        in_specs=[any_spec] * 5 + [smem] * 3,
        out_specs=(any_spec, pl.BlockSpec(memory_space=pltpu.VMEM)),
        scratch_shapes=[
            pltpu.VMEM((TOK, DIM), BF16),
            pltpu.VMEM((TOK, DIM), BF16),
            pltpu.VMEM((TOK, DIM), BF16),
            pltpu.VMEM((TOK, DIM), BF16),
            pltpu.VMEM((2, DIM, FF), BF16),
            pltpu.VMEM((FF, DIM), BF16),
            pltpu.VMEM((2, DIM, HALF), BF16),
            pltpu.VMEM((HALF, DIM), BF16),
            pltpu.VMEM((STEPS, 128, HALF), F32),
            pltpu.VMEM((STEPS, 128, HALF), BF16),
            pltpu.VMEM((6, STEPS, ROWS, HALF), BF16),
            pltpu.VMEM((STEPS, ROWS, HALF), BF16),
            pltpu.VMEM((STEPS, ROWS, HALF), BF16),
            pltpu.VMEM((STEPS, 2, ROWS, HALF), F32),
            pltpu.VMEM((STEPS, ROWS, HALF), F32),
            pltpu.VMEM((3, CHUNKS, 128, FF), BF16),
            pltpu.VMEM((CHUNKS, 128, DIM), F32),
            pltpu.VMEM((CHUNKS, 128, DIM), BF16),
            pltpu.VMEM((6, 64, DIM), BF16),
            pltpu.VMEM((128, DIM), F32),
            pltpu.VMEM((3, 32, DIM), F32),
            dma((6 + CHUNKS,)),
            dma((5,)),
            dma((5,)),
            dma((6, STEPS)),
            dma((6, STEPS)),
            dma((STEPS,)),
            dma((STEPS,)),
            dma((CHUNKS + 1, 8)),
            dma((CHUNKS + 1, 8)),
            dma((6,)),
            dma((6,)),
            dma((3,)),
            dma((3,)),
        ],
        compiler_params=pltpu.CompilerParams(
            collective_id=0, has_side_effects=True, vmem_limit_bytes=56 * 2**20
        ),
        name="exchange",
    )(inputs, out_grad, gate_weight, up_weight, down_weight, gate_mask, up_mask, down_mask)


def grads_kernel(x_ref, og_ref, d_ref, gm, um, dm, ig_ref, gate_out, up_out, down_out, ig_out):
    j = pl.program_id(0)
    ig_out[...] = ig_ref[...]
    for which, mask, out in ((1, gm, gate_out), (2, um, up_out)):
        value = t_product(x_ref[...], d_ref[which])
        for i in range(DIM // BLOCK):
            for k in range(2):
                keep = mask[i, 2 * j + k].astype(F32)
                blk = (slice(i * BLOCK, (i + 1) * BLOCK), slice(k * BLOCK, (k + 1) * BLOCK))
                out[blk] = (value[blk] * keep).astype(BF16)
    value = t_product(d_ref[0], og_ref[...])
    for k in range(2):
        for i in range(DIM // BLOCK):
            keep = dm[2 * j + k, i].astype(F32)
            blk = (slice(k * BLOCK, (k + 1) * BLOCK), slice(i * BLOCK, (i + 1) * BLOCK))
            down_out[blk] = (value[blk] * keep).astype(BF16)


def grads(inputs, out_grad, deltas, gate_mask, up_mask, down_mask, ig):
    smem = pl.BlockSpec(memory_space=pltpu.SMEM)
    whole = pl.BlockSpec((TOK, DIM), lambda j: (0, 0))
    ig_spec = pl.BlockSpec((32, DIM), lambda j: (0, 0))
    return pl.pallas_call(
        grads_kernel,
        grid=(FF // 256,),
        out_shape=(
            jax.ShapeDtypeStruct((DIM, FF), BF16),
            jax.ShapeDtypeStruct((DIM, FF), BF16),
            jax.ShapeDtypeStruct((FF, DIM), BF16),
            jax.ShapeDtypeStruct((32, DIM), BF16),
        ),
        in_specs=[whole, whole, pl.BlockSpec((3, TOK, 256), lambda j: (0, 0, j)), smem, smem, smem, ig_spec],
        out_specs=(
            pl.BlockSpec((DIM, 256), lambda j: (0, j)),
            pl.BlockSpec((DIM, 256), lambda j: (0, j)),
            pl.BlockSpec((256, DIM), lambda j: (j, 0)),
            ig_spec,
        ),
        name="grads",
    )(inputs, out_grad, deltas, gate_mask, up_mask, down_mask, ig)


def shards(inputs, out_grad, gate_weight, up_weight, down_weight, gate_mask, up_mask, down_mask):
    deltas, ig = exchange(inputs, out_grad, gate_weight, up_weight, down_weight, gate_mask, up_mask, down_mask)
    deltas = deltas.reshape(3, TOK, FF)
    gate_grad, up_grad, down_grad, input_grad = grads(inputs, out_grad, deltas, gate_mask, up_mask, down_mask, ig)
    return (input_grad, gate_grad, up_grad, down_grad)


def solution(mesh):
    placed = (
        P(None, "row"),
        P(None, "row"),
        P("row", "col"),
        P("row", "col"),
        P("col", "row"),
        P("row", "col"),
        P("row", "col"),
        P("col", "row"),
    )
    return jax.shard_map(
        shards,
        mesh=mesh,
        in_specs=placed,
        out_specs=(P("col", "row"), P("row", "col"), P("row", "col"), P("col", "row")),
        check_vma=False,
    )
```

```python
import jax
import jax.numpy as jnp
from jax import lax
from jax.experimental import pallas as pl
from jax.experimental.pallas import tpu as pltpu
from jax.sharding import PartitionSpec as P

MESH = pl.DeviceIdType.MESH
F32 = jnp.float32
BF16 = jnp.bfloat16
BLOCK = 128
TOK = 512
DIM = 512
FF = 1792
HALF = FF // 2
CHUNKS = 4
ROWS = 16
STEPS = 3 * CHUNKS

LAG_RING = 1
LAG_FORWARD = 3
LAG_OWN = 5
LAG_FINAL = 9
LAG_RELAY = 11
LAG_CORE = 13
LAG_GRAD = 14
LAG_COL = 16
TURN = 13

R1, R2, R3, L1, L2, L3 = range(6)


def product(left, right):
    return jnp.dot(left, right, preferred_element_type=F32)


def product_t(left, right):
    return lax.dot_general(left, right, (((1,), (1,)), ((), ())), preferred_element_type=F32)


def t_product(left, right):
    return lax.dot_general(left, right, (((0,), (0,)), ((), ())), preferred_element_type=F32)


def exchange_kernel(
    x_hbm, og_hbm, wg_hbm, wu_hbm, wd_hbm, gm, um, dm,
    d_hbm, xt_hbm, ig_out,
    x_own, og_own, xt, w_own, wd_own, core_out, core_in,
    part, send, ring, z_out, z_in, sums, deltas,
    ig, ig_x, ig_z, ig_sum, ig_in,
    local_sem, core_s, core_r, ring_s, ring_r, z_s, z_r, ag_s, ag_r, x_s, x_r, zl_s, zl_r,
):
    row = lax.axis_index("row")
    col = lax.axis_index("col")
    y = row // 4
    h = (row // 2) % 2
    c = row % 2
    x = col // 4
    zl = col % 4
    up = lax.rem(y + 1, 4)
    down = lax.rem(y + 3, 4)
    far = lax.rem(y + 2, 4)

    def ring_dev(yy):
        return (yy * 4 + h * 2 + c, col)

    right = ring_dev(up)
    left = ring_dev(down)
    z_dev = (y * 4 + (1 - h) * 2 + c, col)
    core_dev = (y * 4 + h * 2 + (1 - c), col)
    own_cols = pl.ds(pl.multiple_of(c * HALF, 128), HALF)
    oth_cols = pl.ds(pl.multiple_of((1 - c) * HALF, 128), HALF)

    def x_dev(d):
        return (row, lax.rem(x + d, 4) * 4 + zl)

    def remote(src, dst, ss, rs, dev):
        return pltpu.make_async_remote_copy(
            src_ref=src, dst_ref=dst, send_sem=ss, recv_sem=rs, device_id=dev, device_id_type=MESH
        )

    def chunk(k):
        return lax.rem(k + 2, 4)

    def piece(yy, hh):
        return pl.ds(pl.multiple_of(yy * 32 + hh * ROWS, ROWS), ROWS)

    def half(hh):
        return pl.ds(pl.multiple_of(hh * ROWS, ROWS), ROWS)

    loads = [
        pltpu.make_async_copy(x_hbm, x_own, local_sem.at[0]),
        pltpu.make_async_copy(wg_hbm, w_own.at[0], local_sem.at[1]),
        pltpu.make_async_copy(wu_hbm, w_own.at[1], local_sem.at[2]),
        pltpu.make_async_copy(og_hbm, og_own, local_sem.at[3]),
        pltpu.make_async_copy(wd_hbm, wd_own, local_sem.at[4]),
    ]
    for load in loads:
        load.start()

    bar = pltpu.get_barrier_semaphore()
    friends = [right, left, z_dev, core_dev] + [x_dev(d) for d in (1, 2, 3)]
    friends += [(row, x * 4 + lax.rem(zl + d, 4)) for d in (1, 2, 3)]
    for dev in friends:
        pl.semaphore_signal(bar, inc=1, device_id=dev, device_id_type=MESH)
    pl.semaphore_wait(bar, len(friends))

    def mask_cols(which, mask_ref):
        @pl.loop(0, FF // BLOCK)
        def _(j):
            cols = pl.ds(pl.multiple_of(j * BLOCK, BLOCK), BLOCK)
            for i in range(DIM // BLOCK):
                rows = pl.ds(i * BLOCK, BLOCK)
                keep = jnp.full((BLOCK, BLOCK), mask_ref[i, j].astype(F32), F32).astype(BF16)
                w_own[which, rows, cols] = w_own[which, rows, cols] * keep

    def mask_rows():
        @pl.loop(0, FF // BLOCK)
        def _(j):
            rows = pl.ds(pl.multiple_of(j * BLOCK, BLOCK), BLOCK)
            for i in range(DIM // BLOCK):
                cols = pl.ds(i * BLOCK, BLOCK)
                keep = jnp.full((BLOCK, BLOCK), dm[i, j].astype(F32), F32).astype(BF16)
                wd_own[rows, cols] = wd_own[rows, cols] * keep

    def core_copy(s):
        return remote(core_out.at[s], core_in.at[s], core_s.at[s], core_r.at[s], core_dev)

    def ring_copy(kind, s, yy, hh):
        dev = right if kind in (R1, R2, R3) else left
        return remote(send.at[s, piece(yy, hh)], ring.at[kind, s], ring_s.at[kind, s], ring_r.at[kind, s], dev)

    def ring_early(s):
        return [ring_copy(R1, s, far, 0), ring_copy(L1, s, far, 1), ring_copy(R2, s, up, 1), ring_copy(L2, s, down, 0)]

    def ring_late(s):
        return [ring_copy(R3, s, up, 0), ring_copy(L3, s, down, 1)]

    def z_copy(s):
        return remote(z_out.at[s], z_in.at[s], z_s.at[s], z_r.at[s], z_dev)

    def y_copy(m, k):
        def copy(i, yy, hh, dev):
            ref = deltas.at[m, k, yy, half(hh), own_cols]
            return remote(ref, ref, ag_s.at[m, k, i], ag_r.at[m, k, i], dev)

        return copy

    def pair_copy(m, k, cols):
        ref = deltas.at[m, k, :, :, cols]
        return remote(ref, ref, ag_s.at[m, k, 6], ag_r.at[m, k, 6], core_dev)

    def gather_own(copy):
        copy(0, y, 0, right).start()
        copy(3, y, 1, left).start()
        copy(1, y, 1, right).start()
        copy(2, y, 0, left).start()

    def gather_relay(copy):
        copy(0, down, 0, right).wait_recv()
        copy(4, down, 0, right).start()
        copy(3, up, 1, left).wait_recv()
        copy(5, up, 1, left).start()

    def gather_rest(copy):
        copy(1, down, 1, right).wait_recv()
        copy(2, up, 0, left).wait_recv()
        copy(4, far, 0, right).wait_recv()
        copy(5, far, 1, left).wait_recv()

    def gather_drain(copy):
        for hh in range(2):
            copy(hh, y, hh, right).wait_send()
            copy(2 + hh, y, hh, left).wait_send()
        copy(4, down, 0, right).wait_send()
        copy(5, up, 1, left).wait_send()

    def out_copy(k):
        return pltpu.make_async_copy(
            deltas.at[pl.ds(1, 2), k], d_hbm.at[pl.ds(1, 2), :, chunk(k)], local_sem.at[5 + k]
        )

    def hidden_store(k):
        return pltpu.make_async_copy(deltas.at[0, k], d_hbm.at[0, :, chunk(k)], local_sem.at[10 + k])

    xt_copy = pltpu.make_async_copy(xt, xt_hbm, local_sem.at[9])

    def x_copy(k, d):
        return remote(
            ig.at[k, lax.rem(x + d, 4)], ig_x.at[k, d - 1], x_s.at[k, d - 1], x_r.at[k, d - 1], x_dev(d)
        )

    def zl_copy(k):
        slot = lax.rem(zl - chunk(k) + 7, 4)
        return remote(ig_z.at[k], ig_in.at[slot], zl_s.at[k], zl_r.at[slot], (row, x * 4 + chunk(k)))

    def reduce_col(k):
        total = ig[k, x]
        for d in (1, 2, 3):
            x_copy(k, d).wait_recv()
            total = total + ig_x[k, d - 1]

        @pl.when(zl == chunk(k))
        def _():
            ig_sum[...] = total

        @pl.when(zl != chunk(k))
        def _():
            ig_z[k] = total.astype(BF16)
            zl_copy(k).start()

    def at_chunk(s, lag, fn, count=CHUNKS):
        @pl.when((s >= lag + 2) & (s < 3 * count + lag) & (lax.rem(s + 3 * 16 - lag, 3) == 2))
        def _():
            fn((s - lag) // 3)

    @pl.loop(0, STEPS + LAG_COL)
    def _(s):
        @pl.when(s < STEPS)
        def _():
            m = lax.rem(s, 3)
            t = chunk(s // 3)

            @pl.when(s == 0)
            def _():
                loads[0].wait()
                loads[1].wait()
                mask_cols(0, gm)

            @pl.when(s == 1)
            def _():
                loads[2].wait()
                mask_cols(1, um)

            @pl.when(s == 2)
            def _():
                loads[3].wait()
                loads[4].wait()
                mask_rows()

            @pl.when(m < 2)
            def _():
                rows = x_own[:, t].reshape(128, DIM)
                core_out[s] = product(rows, w_own[m, :, oth_cols])
                core_copy(s).start()
                part[s] = product(rows, w_own[m, :, own_cols])

            @pl.when(m == 2)
            def _():
                rows = og_own[:, t].reshape(128, DIM)
                core_out[s] = product_t(rows, wd_own[oth_cols, :])
                core_copy(s).start()
                part[s] = product_t(rows, wd_own[own_cols, :])

        @pl.when((s >= LAG_RING) & (s < STEPS + LAG_RING))
        def _():
            n = s - LAG_RING
            core_copy(n).wait_recv()
            value = part[n] + core_in[n]
            part[n] = value
            send[n] = value.astype(BF16)
            for copy in ring_early(n):
                copy.start()

        @pl.when((s >= LAG_FORWARD) & (s < STEPS + LAG_FORWARD))
        def _():
            n = s - LAG_FORWARD
            first = ring_early(n)[:2]
            onward = ring_late(n)
            first[0].wait_recv()
            send[n, piece(up, 0)] = (part[n, piece(up, 0)] + ring[R1, n].astype(F32)).astype(BF16)
            onward[0].start()
            first[1].wait_recv()
            send[n, piece(down, 1)] = (part[n, piece(down, 1)] + ring[L1, n].astype(F32)).astype(BF16)
            onward[1].start()

        @pl.when((s >= LAG_OWN) & (s < STEPS + LAG_OWN))
        def _():
            n = s - LAG_OWN
            for copy in ring_early(n)[2:] + ring_late(n):
                copy.wait_recv()
            first = part[n, piece(y, 0)] + ring[R3, n].astype(F32) + ring[L2, n].astype(F32)
            second = part[n, piece(y, 1)] + ring[L3, n].astype(F32) + ring[R2, n].astype(F32)
            sums[n, 0:ROWS] = first
            sums[n, ROWS : 2 * ROWS] = second
            z_out[n, 0:ROWS] = first.astype(BF16)
            z_out[n, ROWS : 2 * ROWS] = second.astype(BF16)
            z_copy(n).start()

        @pl.when((s >= LAG_FINAL) & (s < STEPS + LAG_FINAL))
        def _():
            n = s - LAG_FINAL
            z_copy(n).wait_recv()
            sums[n] = sums[n] + z_in[n].astype(F32)

        @pl.when(s == TURN)
        def _():
            xt[...] = x_own[...].reshape(TOK, DIM).T
            xt_copy.start()

        def pointwise(k):
            gate = sums[3 * k]
            upv = sums[3 * k + 1]
            back = sums[3 * k + 2]
            sig = jax.nn.sigmoid(gate)
            slope = sig * (1.0 + gate * (1.0 - sig))
            deltas[1, k, y, :, own_cols] = (back * upv * slope).astype(BF16)
            gather_own(y_copy(1, k))
            deltas[2, k, y, :, own_cols] = (back * gate * sig).astype(BF16)
            gather_own(y_copy(2, k))
            deltas[0, k, y, :, own_cols] = (gate * sig * upv).astype(BF16)

        def relay(k):
            gather_relay(y_copy(1, k))
            gather_relay(y_copy(2, k))
            gather_own(y_copy(0, k))

        def to_core(k):
            for m in (1, 2):
                gather_rest(y_copy(m, k))
                pair_copy(m, k, own_cols).start()
            gather_relay(y_copy(0, k))

        def grad(k):
            pair_copy(1, k, oth_cols).wait_recv()
            value = product_t(deltas[1, k].reshape(128, FF), w_own[0])
            pair_copy(2, k, oth_cols).wait_recv()
            value = value + product_t(deltas[2, k].reshape(128, FF), w_own[1])
            ig[k] = value.reshape(4, 32, DIM)
            for d in (2, 1, 3):
                x_copy(k, d).start()
            out_copy(k).start()
            gather_rest(y_copy(0, k))
            pair_copy(0, k, own_cols).start()

        def finish(k):
            pair_copy(0, k, oth_cols).wait_recv()
            hidden_store(k).start()
            reduce_col(k)

        at_chunk(s, LAG_FINAL, pointwise)
        at_chunk(s, LAG_RELAY, relay)
        at_chunk(s, LAG_CORE, to_core)
        at_chunk(s, LAG_GRAD, grad)
        at_chunk(s, LAG_COL, finish)

    total = ig_sum[...]
    for i in range(3):
        remote(ig_z.at[0], ig_in.at[i], zl_s.at[0], zl_r.at[i], core_dev).wait_recv()
        total = total + ig_in[i].astype(F32)
    ig_out[...] = total.astype(BF16)

    @pl.loop(0, STEPS)
    def _(s):
        core_copy(s).wait_send()
        for copy in ring_early(s) + ring_late(s):
            copy.wait_send()
        z_copy(s).wait_send()

    @pl.loop(0, CHUNKS)
    def _(k):
        for m in range(3):
            gather_drain(y_copy(m, k))
            pair_copy(m, k, own_cols).wait_send()
        for d in (1, 2, 3):
            x_copy(k, d).wait_send()

        @pl.when(zl != chunk(k))
        def _():
            zl_copy(k).wait_send()

        out_copy(k).wait()
        hidden_store(k).wait()

    xt_copy.wait()


def exchange(inputs, out_grad, gate_weight, up_weight, down_weight, gate_mask, up_mask, down_mask):
    any_spec = pl.BlockSpec(memory_space=pl.ANY)
    smem = pl.BlockSpec(memory_space=pltpu.SMEM)
    dma = pltpu.SemaphoreType.DMA
    return pl.pallas_call(
        exchange_kernel,
        out_shape=(
            jax.ShapeDtypeStruct((3, 4, CHUNKS, 32, FF), BF16),
            jax.ShapeDtypeStruct((DIM, TOK), BF16),
            jax.ShapeDtypeStruct((32, DIM), BF16),
        ),
        in_specs=[any_spec] * 5 + [smem] * 3,
        out_specs=(any_spec, any_spec, pl.BlockSpec(memory_space=pltpu.VMEM)),
        scratch_shapes=[
            pltpu.VMEM((4, CHUNKS, 32, DIM), BF16),
            pltpu.VMEM((4, CHUNKS, 32, DIM), BF16),
            pltpu.VMEM((DIM, TOK), BF16),
            pltpu.VMEM((2, DIM, FF), BF16),
            pltpu.VMEM((FF, DIM), BF16),
            pltpu.VMEM((STEPS, 128, HALF), F32),
            pltpu.VMEM((STEPS, 128, HALF), F32),
            pltpu.VMEM((STEPS, 128, HALF), F32),
            pltpu.VMEM((STEPS, 128, HALF), BF16),
            pltpu.VMEM((6, STEPS, ROWS, HALF), BF16),
            pltpu.VMEM((STEPS, 2 * ROWS, HALF), BF16),
            pltpu.VMEM((STEPS, 2 * ROWS, HALF), BF16),
            pltpu.VMEM((STEPS, 2 * ROWS, HALF), F32),
            pltpu.VMEM((3, CHUNKS, 4, 32, FF), BF16),
            pltpu.VMEM((CHUNKS, 4, 32, DIM), F32),
            pltpu.VMEM((CHUNKS, 3, 32, DIM), F32),
            pltpu.VMEM((CHUNKS, 32, DIM), BF16),
            pltpu.VMEM((32, DIM), F32),
            pltpu.VMEM((3, 32, DIM), BF16),
            dma((14,)),
            dma((STEPS,)),
            dma((STEPS,)),
            dma((6, STEPS)),
            dma((6, STEPS)),
            dma((STEPS,)),
            dma((STEPS,)),
            dma((3, CHUNKS, 7)),
            dma((3, CHUNKS, 7)),
            dma((CHUNKS, 3)),
            dma((CHUNKS, 3)),
            dma((CHUNKS,)),
            dma((3,)),
        ],
        compiler_params=pltpu.CompilerParams(
            collective_id=0, has_side_effects=True, vmem_limit_bytes=58 * 2**20
        ),
        name="exchange",
    )(
        inputs.reshape(4, CHUNKS, 32, DIM),
        out_grad.reshape(4, CHUNKS, 32, DIM),
        gate_weight,
        up_weight,
        down_weight,
        gate_mask,
        up_mask,
        down_mask.T,
    )


def grads_kernel(
    xt_hbm, og_hbm, d_hbm, gm, um, dm, ig_ref, gate_hbm, up_hbm, down_hbm, ig_out, xt, og, d, cols_out, rows_out, sem_in, sem_out
):
    loads = [
        pltpu.make_async_copy(xt_hbm, xt, sem_in.at[0]),
        pltpu.make_async_copy(d_hbm.at[1], d.at[1], sem_in.at[1]),
        pltpu.make_async_copy(d_hbm.at[2], d.at[2], sem_in.at[2]),
        pltpu.make_async_copy(og_hbm, og, sem_in.at[3]),
        pltpu.make_async_copy(d_hbm.at[0], d.at[0], sem_in.at[4]),
    ]
    for load in loads:
        load.start()
    ig_out[...] = ig_ref[...]
    loads[0].wait()
    stores = [
        pltpu.make_async_copy(cols_out.at[0], gate_hbm, sem_out.at[0]),
        pltpu.make_async_copy(cols_out.at[1], up_hbm, sem_out.at[1]),
    ]
    for which, mask in ((1, gm), (2, um)):
        loads[which].wait()

        @pl.loop(0, FF // 256)
        def _(j):
            value = product(xt[...], d[which, :, pl.ds(pl.multiple_of(j * 256, 256), 256)])
            for k in range(2):
                cols = pl.ds(pl.multiple_of(j * 256 + k * BLOCK, BLOCK), BLOCK)
                for i in range(DIM // BLOCK):
                    rows = slice(i * BLOCK, (i + 1) * BLOCK)
                    keep = mask[i, 2 * j + k].astype(F32)
                    part = value[rows, k * BLOCK : (k + 1) * BLOCK] * keep
                    cols_out[which - 1, rows, cols] = part.astype(BF16)

        stores[which - 1].start()
    loads[3].wait()
    loads[4].wait()

    def store_rows(j):
        rows = pl.ds(pl.multiple_of(j * 256, 256), 256)
        return pltpu.make_async_copy(rows_out.at[rows], down_hbm.at[rows], sem_out.at[2 + j])

    @pl.loop(0, FF // 256)
    def _(j):
        value = t_product(d[0, :, pl.ds(pl.multiple_of(j * 256, 256), 256)], og[...])
        for k in range(2):
            rows = pl.ds(pl.multiple_of(j * 256 + k * BLOCK, BLOCK), BLOCK)
            for i in range(DIM // BLOCK):
                cols = slice(i * BLOCK, (i + 1) * BLOCK)
                keep = dm[i, 2 * j + k].astype(F32)
                part = value[k * BLOCK : (k + 1) * BLOCK, cols] * keep
                rows_out[rows, cols] = part.astype(BF16)
        store_rows(j).start()

    for store in stores:
        store.wait()
    for j in range(FF // 256):
        store_rows(j).wait()


def grads(turned, out_grad, deltas, gate_mask, up_mask, down_mask, ig):
    any_spec = pl.BlockSpec(memory_space=pl.ANY)
    smem = pl.BlockSpec(memory_space=pltpu.SMEM)
    vmem = pl.BlockSpec(memory_space=pltpu.VMEM)
    return pl.pallas_call(
        grads_kernel,
        out_shape=(
            jax.ShapeDtypeStruct((DIM, FF), BF16),
            jax.ShapeDtypeStruct((DIM, FF), BF16),
            jax.ShapeDtypeStruct((FF, DIM), BF16),
            jax.ShapeDtypeStruct((32, DIM), BF16),
        ),
        in_specs=[any_spec, any_spec, any_spec, smem, smem, smem, vmem],
        out_specs=(any_spec, any_spec, any_spec, vmem),
        scratch_shapes=[
            pltpu.VMEM((DIM, TOK), BF16),
            pltpu.VMEM((TOK, DIM), BF16),
            pltpu.VMEM((3, TOK, FF), BF16),
            pltpu.VMEM((2, DIM, FF), BF16),
            pltpu.VMEM((FF, DIM), BF16),
            pltpu.SemaphoreType.DMA((5,)),
            pltpu.SemaphoreType.DMA((2 + FF // 256,)),
        ],
        compiler_params=pltpu.CompilerParams(vmem_limit_bytes=62 * 2**20),
        name="grads",
    )(turned, out_grad, deltas, gate_mask, up_mask, down_mask.T, ig)


def shards(inputs, out_grad, gate_weight, up_weight, down_weight, gate_mask, up_mask, down_mask):
    deltas, turned, ig = exchange(inputs, out_grad, gate_weight, up_weight, down_weight, gate_mask, up_mask, down_mask)
    deltas = deltas.reshape(3, TOK, FF)
    gate_grad, up_grad, down_grad, input_grad = grads(turned, out_grad, deltas, gate_mask, up_mask, down_mask, ig)
    return (input_grad, gate_grad, up_grad, down_grad)


def solution(mesh):
    placed = (
        P(None, "row"),
        P(None, "row"),
        P("row", "col"),
        P("row", "col"),
        P("col", "row"),
        P("row", "col"),
        P("row", "col"),
        P("col", "row"),
    )
    return jax.shard_map(
        shards,
        mesh=mesh,
        in_specs=placed,
        out_specs=(P("col", "row"), P("row", "col"), P("row", "col"), P("col", "row")),
        check_vma=False,
    )
```

```python
import jax
import jax.numpy as jnp
from jax import lax
from jax.experimental import pallas as pl
from jax.experimental.pallas import tpu as pltpu
from jax.sharding import PartitionSpec as P

MESH = pl.DeviceIdType.MESH
F32 = jnp.float32
BF16 = jnp.bfloat16
BLOCK = 128
TOK = 512
DIM = 512
FF = 1792
HALF = FF // 2
CHUNKS = 4
ROWS = 64 // CHUNKS
GROUP = 2 * ROWS
SPAN = 4 * GROUP
STEPS = 3 * CHUNKS

LAG_RING = 1
LAG_FORWARD = 3
LAG_OWN = 5
LAG_FINAL = 8
LAG_RELAY = 10
LAG_CORE = 12
LAG_GRAD = 13
LAG_COL = 15
TURN = 13

R1, R2, R3, L1, L2, L3 = range(6)


def product(left, right):
    return jnp.dot(left, right, preferred_element_type=F32)


def product_t(left, right):
    return lax.dot_general(left, right, (((1,), (1,)), ((), ())), preferred_element_type=F32)


def t_product(left, right):
    return lax.dot_general(left, right, (((0,), (0,)), ((), ())), preferred_element_type=F32)


def exchange_kernel(
    x_hbm, og_hbm, wg_hbm, wu_hbm, wd_hbm, gm, um, dm,
    d_hbm, xt_hbm, ig_out,
    x_own, og_own, xt, w_own, wd_own, core_out, core_in,
    part, send, ring, z_out, z_in, sums, deltas,
    ig, ig_x, ig_z, ig_sum, ig_in,
    local_sem, core_s, core_r, ring_s, ring_r, z_s, z_r, ag_s, ag_r, x_s, x_r, zl_s, zl_r,
):
    row = lax.axis_index("row")
    col = lax.axis_index("col")
    y = row // 4
    h = (row // 2) % 2
    c = row % 2
    x = col // 4
    zl = col % 4
    up = lax.rem(y + 1, 4)
    down = lax.rem(y + 3, 4)
    far = lax.rem(y + 2, 4)

    def ring_dev(yy):
        return (yy * 4 + h * 2 + c, col)

    right = ring_dev(up)
    left = ring_dev(down)
    z_dev = (y * 4 + (1 - h) * 2 + c, col)
    core_dev = (y * 4 + h * 2 + (1 - c), col)
    own_cols = pl.ds(pl.multiple_of(c * HALF, 128), HALF)
    oth_cols = pl.ds(pl.multiple_of((1 - c) * HALF, 128), HALF)

    def x_dev(d):
        return (row, lax.rem(x + d, 4) * 4 + zl)

    def remote(src, dst, ss, rs, dev):
        return pltpu.make_async_remote_copy(
            src_ref=src, dst_ref=dst, send_sem=ss, recv_sem=rs, device_id=dev, device_id_type=MESH
        )

    def chunk(k):
        return lax.rem(k + CHUNKS // 2, CHUNKS)

    def owner(k):
        return chunk(k) // (CHUNKS // 4)

    def piece(yy, hh):
        return pl.ds(pl.multiple_of(yy * GROUP + hh * ROWS, ROWS), ROWS)

    def half(hh):
        return pl.ds(pl.multiple_of(hh * ROWS, ROWS), ROWS)

    loads = [
        pltpu.make_async_copy(x_hbm, x_own, local_sem.at[0]),
        pltpu.make_async_copy(wg_hbm.at[:, oth_cols], w_own.at[0, :, oth_cols], local_sem.at[1]),
        pltpu.make_async_copy(wg_hbm.at[:, own_cols], w_own.at[0, :, own_cols], local_sem.at[5]),
        pltpu.make_async_copy(wu_hbm, w_own.at[1], local_sem.at[2]),
        pltpu.make_async_copy(og_hbm, og_own, local_sem.at[3]),
        pltpu.make_async_copy(wd_hbm, wd_own, local_sem.at[4]),
    ]
    for load in loads:
        load.start()

    bar = pltpu.get_barrier_semaphore()
    friends = [right, left, z_dev, core_dev] + [x_dev(d) for d in (1, 2, 3)]
    friends += [(row, x * 4 + lax.rem(zl + d, 4)) for d in (1, 2, 3)]
    for dev in friends:
        pl.semaphore_signal(bar, inc=1, device_id=dev, device_id_type=MESH)
    pl.semaphore_wait(bar, len(friends))

    def mask_cols(which, mask_ref, first, count):
        @pl.loop(0, count * HALF // BLOCK)
        def _(n):
            j = first * (HALF // BLOCK) + n
            cols = pl.ds(pl.multiple_of(j * BLOCK, BLOCK), BLOCK)
            for i in range(DIM // BLOCK):
                rows = pl.ds(i * BLOCK, BLOCK)
                keep = jnp.full((BLOCK, BLOCK), mask_ref[i, j].astype(F32), F32).astype(BF16)
                w_own[which, rows, cols] = w_own[which, rows, cols] * keep

    def mask_rows():
        @pl.loop(0, FF // BLOCK)
        def _(j):
            rows = pl.ds(pl.multiple_of(j * BLOCK, BLOCK), BLOCK)
            for i in range(DIM // BLOCK):
                cols = pl.ds(i * BLOCK, BLOCK)
                keep = jnp.full((BLOCK, BLOCK), dm[i, j].astype(F32), F32).astype(BF16)
                wd_own[rows, cols] = wd_own[rows, cols] * keep

    def core_copy(s):
        return remote(core_out.at[s], core_in.at[s], core_s.at[s], core_r.at[s], core_dev)

    def ring_copy(kind, s, yy, hh):
        dev = right if kind in (R1, R2, R3) else left
        return remote(send.at[s, piece(yy, hh)], ring.at[kind, s], ring_s.at[kind, s], ring_r.at[kind, s], dev)

    def ring_early(s):
        return [ring_copy(R1, s, far, 0), ring_copy(L1, s, far, 1), ring_copy(R2, s, up, 1), ring_copy(L2, s, down, 0)]

    def ring_late(s):
        return [ring_copy(R3, s, up, 0), ring_copy(L3, s, down, 1)]

    def z_copy(s):
        return remote(z_out.at[s], z_in.at[s], z_s.at[s], z_r.at[s], z_dev)

    def y_copy(m, k):
        def copy(i, yy, hh, dev):
            ref = deltas.at[m, k, yy, half(hh), own_cols]
            return remote(ref, ref, ag_s.at[m, k, i], ag_r.at[m, k, i], dev)

        return copy

    def pair_copy(m, k, cols):
        ref = deltas.at[m, k, :, :, cols]
        return remote(ref, ref, ag_s.at[m, k, 6], ag_r.at[m, k, 6], core_dev)

    def gather_own(*copies):
        for copy in copies:
            copy(0, y, 0, right).start()
            copy(3, y, 1, left).start()
        for copy in copies:
            copy(1, y, 1, right).start()
            copy(2, y, 0, left).start()

    def gather_relay(copy):
        copy(0, down, 0, right).wait_recv()
        copy(4, down, 0, right).start()
        copy(3, up, 1, left).wait_recv()
        copy(5, up, 1, left).start()

    def gather_rest(copy):
        copy(1, down, 1, right).wait_recv()
        copy(2, up, 0, left).wait_recv()
        copy(4, far, 0, right).wait_recv()
        copy(5, far, 1, left).wait_recv()

    def gather_drain(copy):
        for hh in range(2):
            copy(hh, y, hh, right).wait_send()
            copy(2 + hh, y, hh, left).wait_send()
        copy(4, down, 0, right).wait_send()
        copy(5, up, 1, left).wait_send()

    def out_copy(k):
        return pltpu.make_async_copy(
            deltas.at[pl.ds(1, 2), k], d_hbm.at[pl.ds(1, 2), :, chunk(k)], local_sem.at[7 + k]
        )

    def hidden_store(k):
        return pltpu.make_async_copy(deltas.at[0, k], d_hbm.at[0, :, chunk(k)], local_sem.at[7 + CHUNKS + k])

    xt_copy = pltpu.make_async_copy(xt, xt_hbm, local_sem.at[6])

    def x_copy(k, d):
        return remote(
            ig.at[k, lax.rem(x + d, 4)], ig_x.at[k, d - 1], x_s.at[k, d - 1], x_r.at[k, d - 1], x_dev(d)
        )

    def zl_copy(k):
        slot = lax.rem(zl - owner(k) + 7, 4)
        part_of = lax.rem(chunk(k), CHUNKS // 4)
        return remote(
            ig_z.at[k], ig_in.at[part_of, slot], zl_s.at[k], zl_r.at[part_of, slot], (row, x * 4 + owner(k))
        )

    def reduce_col(k):
        total = ig[k, x]
        for d in (1, 2, 3):
            x_copy(k, d).wait_recv()
            total = total + ig_x[k, d - 1]

        @pl.when(zl == owner(k))
        def _():
            ig_sum[lax.rem(chunk(k), CHUNKS // 4)] = total

        @pl.when(zl != owner(k))
        def _():
            ig_z[k] = total.astype(BF16)
            zl_copy(k).start()

    def drain(k):
        for m in range(3):
            gather_drain(y_copy(m, k))
            pair_copy(m, k, own_cols).wait_send()
        for d in (1, 2, 3):
            x_copy(k, d).wait_send()

        @pl.when(zl != owner(k))
        def _():
            zl_copy(k).wait_send()

        out_copy(k).wait()
        hidden_store(k).wait()

    def at_chunk(s, lag, fn, count=CHUNKS):
        @pl.when((s >= lag + 2) & (s < 3 * count + lag) & (lax.rem(s + 3 * 32 - lag, 3) == 2))
        def _():
            fn((s - lag) // 3)

    @pl.loop(0, STEPS + LAG_COL)
    def _(s):
        @pl.when(s < STEPS)
        def _():
            m = lax.rem(s, 3)
            t = chunk(s // 3)

            @pl.when(s == 0)
            def _():
                loads[0].wait()
                loads[1].wait()
                mask_cols(0, gm, 1 - c, 1)

            @pl.when(s == 1)
            def _():
                loads[3].wait()
                mask_cols(1, um, 0, 2)

            @pl.when(s == 2)
            def _():
                loads[4].wait()
                loads[5].wait()
                mask_rows()

            @pl.when(m < 2)
            def _():
                rows = x_own[:, t].reshape(SPAN, DIM)
                core_out[s] = product(rows, w_own[m, :, oth_cols])
                core_copy(s).start()

                @pl.when(s == 0)
                def _():
                    loads[2].wait()
                    mask_cols(0, gm, c, 1)

                part[s] = product(rows, w_own[m, :, own_cols])

            @pl.when(m == 2)
            def _():
                rows = og_own[:, t].reshape(SPAN, DIM)
                core_out[s] = product_t(rows, wd_own[oth_cols, :])
                core_copy(s).start()
                part[s] = product_t(rows, wd_own[own_cols, :])

        @pl.when((s >= LAG_RING) & (s < STEPS + LAG_RING))
        def _():
            n = s - LAG_RING
            core_copy(n).wait_recv()
            value = part[n] + core_in[n]
            part[n] = value
            send[n] = value.astype(BF16)
            for copy in ring_early(n):
                copy.start()

        @pl.when((s >= LAG_FORWARD) & (s < STEPS + LAG_FORWARD))
        def _():
            n = s - LAG_FORWARD
            first = ring_early(n)[:2]
            onward = ring_late(n)
            first[0].wait_recv()
            send[n, piece(up, 0)] = (part[n, piece(up, 0)] + ring[R1, n].astype(F32)).astype(BF16)
            onward[0].start()
            first[1].wait_recv()
            send[n, piece(down, 1)] = (part[n, piece(down, 1)] + ring[L1, n].astype(F32)).astype(BF16)
            onward[1].start()

        @pl.when((s >= LAG_OWN) & (s < STEPS + LAG_OWN))
        def _():
            n = s - LAG_OWN
            for copy in ring_early(n)[2:] + ring_late(n):
                copy.wait_recv()
            first = part[n, piece(y, 0)] + ring[R3, n].astype(F32) + ring[L2, n].astype(F32)
            second = part[n, piece(y, 1)] + ring[L3, n].astype(F32) + ring[R2, n].astype(F32)
            sums[n, 0:ROWS] = first
            sums[n, ROWS : 2 * ROWS] = second
            z_out[n, 0:ROWS] = first.astype(BF16)
            z_out[n, ROWS : 2 * ROWS] = second.astype(BF16)
            z_copy(n).start()

        @pl.when((s >= LAG_FINAL) & (s < STEPS + LAG_FINAL))
        def _():
            n = s - LAG_FINAL
            z_copy(n).wait_recv()
            sums[n] = sums[n] + z_in[n].astype(F32)
            core_copy(n).wait_send()
            for copy in ring_early(n) + ring_late(n):
                copy.wait_send()
            z_copy(n).wait_send()

        @pl.when(s == TURN)
        def _():
            xt[...] = x_own[...].reshape(TOK, DIM).T
            xt_copy.start()

        def pointwise(k):
            gate = sums[3 * k]
            upv = sums[3 * k + 1]
            back = sums[3 * k + 2]
            sig = jax.nn.sigmoid(gate)
            slope = sig * (1.0 + gate * (1.0 - sig))
            deltas[1, k, y, :, own_cols] = (back * upv * slope).astype(BF16)
            deltas[2, k, y, :, own_cols] = (back * gate * sig).astype(BF16)
            gather_own(y_copy(1, k), y_copy(2, k))
            deltas[0, k, y, :, own_cols] = (gate * sig * upv).astype(BF16)

        def relay(k):
            gather_relay(y_copy(1, k))
            gather_relay(y_copy(2, k))
            gather_own(y_copy(0, k))

        def to_core(k):
            for m in (1, 2):
                gather_rest(y_copy(m, k))
                pair_copy(m, k, own_cols).start()
            gather_relay(y_copy(0, k))

        def grad(k):
            pair_copy(1, k, oth_cols).wait_recv()
            value = product_t(deltas[1, k].reshape(SPAN, FF), w_own[0])
            pair_copy(2, k, oth_cols).wait_recv()
            value = value + product_t(deltas[2, k].reshape(SPAN, FF), w_own[1])
            ig[k] = value.reshape(4, GROUP, DIM)
            for d in (2, 1, 3):
                x_copy(k, d).start()
            out_copy(k).start()
            gather_rest(y_copy(0, k))
            pair_copy(0, k, own_cols).start()

        def finish(k):
            pair_copy(0, k, oth_cols).wait_recv()
            hidden_store(k).start()
            reduce_col(k)

            @pl.when(k > 0)
            def _():
                drain(k - 1)

        at_chunk(s, LAG_FINAL, pointwise)
        at_chunk(s, LAG_RELAY, relay)
        at_chunk(s, LAG_CORE, to_core)
        at_chunk(s, LAG_GRAD, grad)
        at_chunk(s, LAG_COL, finish)

    for part_of in range(CHUNKS // 4):
        total = ig_sum[part_of]
        for i in range(3):
            remote(
                ig_z.at[0], ig_in.at[part_of, i], zl_s.at[0], zl_r.at[part_of, i], core_dev
            ).wait_recv()
            total = total + ig_in[part_of, i].astype(F32)
        ig_out[pl.ds(part_of * GROUP, GROUP)] = total.astype(BF16)

    drain(CHUNKS - 1)
    xt_copy.wait()


def exchange(inputs, out_grad, gate_weight, up_weight, down_weight, gate_mask, up_mask, down_mask):
    any_spec = pl.BlockSpec(memory_space=pl.ANY)
    smem = pl.BlockSpec(memory_space=pltpu.SMEM)
    dma = pltpu.SemaphoreType.DMA
    return pl.pallas_call(
        exchange_kernel,
        out_shape=(
            jax.ShapeDtypeStruct((3, 4, CHUNKS, GROUP, FF), BF16),
            jax.ShapeDtypeStruct((DIM, TOK), BF16),
            jax.ShapeDtypeStruct((32, DIM), BF16),
        ),
        in_specs=[any_spec] * 5 + [smem] * 3,
        out_specs=(any_spec, any_spec, pl.BlockSpec(memory_space=pltpu.VMEM)),
        scratch_shapes=[
            pltpu.VMEM((4, CHUNKS, GROUP, DIM), BF16),
            pltpu.VMEM((4, CHUNKS, GROUP, DIM), BF16),
            pltpu.VMEM((DIM, TOK), BF16),
            pltpu.VMEM((2, DIM, FF), BF16),
            pltpu.VMEM((FF, DIM), BF16),
            pltpu.VMEM((STEPS, SPAN, HALF), F32),
            pltpu.VMEM((STEPS, SPAN, HALF), F32),
            pltpu.VMEM((STEPS, SPAN, HALF), F32),
            pltpu.VMEM((STEPS, SPAN, HALF), BF16),
            pltpu.VMEM((6, STEPS, ROWS, HALF), BF16),
            pltpu.VMEM((STEPS, 2 * ROWS, HALF), BF16),
            pltpu.VMEM((STEPS, 2 * ROWS, HALF), BF16),
            pltpu.VMEM((STEPS, 2 * ROWS, HALF), F32),
            pltpu.VMEM((3, CHUNKS, 4, GROUP, FF), BF16),
            pltpu.VMEM((CHUNKS, 4, GROUP, DIM), F32),
            pltpu.VMEM((CHUNKS, 3, GROUP, DIM), F32),
            pltpu.VMEM((CHUNKS, GROUP, DIM), BF16),
            pltpu.VMEM((CHUNKS // 4, GROUP, DIM), F32),
            pltpu.VMEM((CHUNKS // 4, 3, GROUP, DIM), BF16),
            dma((7 + 2 * CHUNKS,)),
            dma((STEPS,)),
            dma((STEPS,)),
            dma((6, STEPS)),
            dma((6, STEPS)),
            dma((STEPS,)),
            dma((STEPS,)),
            dma((3, CHUNKS, 7)),
            dma((3, CHUNKS, 7)),
            dma((CHUNKS, 3)),
            dma((CHUNKS, 3)),
            dma((CHUNKS,)),
            dma((CHUNKS // 4, 3)),
        ],
        compiler_params=pltpu.CompilerParams(
            collective_id=0, has_side_effects=True, vmem_limit_bytes=58 * 2**20
        ),
        name="exchange",
    )(
        inputs.reshape(4, CHUNKS, GROUP, DIM),
        out_grad.reshape(4, CHUNKS, GROUP, DIM),
        gate_weight,
        up_weight,
        down_weight,
        gate_mask,
        up_mask,
        down_mask.T,
    )


def grads_kernel(
    xt_hbm, og_hbm, d_hbm, gm, um, dm, ig_ref, gate_hbm, up_hbm, down_hbm, ig_out, xt, og, d, cols_out, rows_out, sem_in, sem_out
):
    loads = [
        pltpu.make_async_copy(xt_hbm, xt, sem_in.at[0]),
        pltpu.make_async_copy(d_hbm.at[1], d.at[1], sem_in.at[1]),
        pltpu.make_async_copy(d_hbm.at[2], d.at[2], sem_in.at[2]),
        pltpu.make_async_copy(og_hbm, og, sem_in.at[3]),
        pltpu.make_async_copy(d_hbm.at[0], d.at[0], sem_in.at[4]),
    ]
    for load in loads:
        load.start()
    ig_out[...] = ig_ref[...]
    loads[0].wait()
    stores = [
        pltpu.make_async_copy(cols_out.at[0], gate_hbm, sem_out.at[0]),
        pltpu.make_async_copy(cols_out.at[1], up_hbm, sem_out.at[1]),
    ]
    for which, mask in ((1, gm), (2, um)):
        loads[which].wait()

        for j in range(FF // 256):
            value = product(xt[...], d[which, :, j * 256 : (j + 1) * 256])
            for k in range(2):
                cols = pl.ds(j * 256 + k * BLOCK, BLOCK)
                for i in range(DIM // BLOCK):
                    rows = slice(i * BLOCK, (i + 1) * BLOCK)
                    keep = mask[i, 2 * j + k].astype(F32)
                    part = value[rows, k * BLOCK : (k + 1) * BLOCK] * keep
                    cols_out[which - 1, rows, cols] = part.astype(BF16)

        stores[which - 1].start()
    loads[3].wait()
    loads[4].wait()

    def store_rows(j):
        rows = pl.ds(j * 256, 256)
        return pltpu.make_async_copy(rows_out.at[rows], down_hbm.at[rows], sem_out.at[2 + j])

    for j in range(FF // 256):
        value = t_product(d[0, :, j * 256 : (j + 1) * 256], og[...])
        for k in range(2):
            rows = pl.ds(j * 256 + k * BLOCK, BLOCK)
            for i in range(DIM // BLOCK):
                cols = slice(i * BLOCK, (i + 1) * BLOCK)
                keep = dm[i, 2 * j + k].astype(F32)
                part = value[k * BLOCK : (k + 1) * BLOCK, cols] * keep
                rows_out[rows, cols] = part.astype(BF16)
        store_rows(j).start()

    for store in stores:
        store.wait()
    for j in range(FF // 256):
        store_rows(j).wait()


def grads(turned, out_grad, deltas, gate_mask, up_mask, down_mask, ig):
    any_spec = pl.BlockSpec(memory_space=pl.ANY)
    smem = pl.BlockSpec(memory_space=pltpu.SMEM)
    vmem = pl.BlockSpec(memory_space=pltpu.VMEM)
    return pl.pallas_call(
        grads_kernel,
        out_shape=(
            jax.ShapeDtypeStruct((DIM, FF), BF16),
            jax.ShapeDtypeStruct((DIM, FF), BF16),
            jax.ShapeDtypeStruct((FF, DIM), BF16),
            jax.ShapeDtypeStruct((32, DIM), BF16),
        ),
        in_specs=[any_spec, any_spec, any_spec, smem, smem, smem, vmem],
        out_specs=(any_spec, any_spec, any_spec, vmem),
        scratch_shapes=[
            pltpu.VMEM((DIM, TOK), BF16),
            pltpu.VMEM((TOK, DIM), BF16),
            pltpu.VMEM((3, TOK, FF), BF16),
            pltpu.VMEM((2, DIM, FF), BF16),
            pltpu.VMEM((FF, DIM), BF16),
            pltpu.SemaphoreType.DMA((5,)),
            pltpu.SemaphoreType.DMA((2 + FF // 256,)),
        ],
        compiler_params=pltpu.CompilerParams(vmem_limit_bytes=62 * 2**20),
        name="grads",
    )(turned, out_grad, deltas, gate_mask, up_mask, down_mask.T, ig)


def shards(inputs, out_grad, gate_weight, up_weight, down_weight, gate_mask, up_mask, down_mask):
    deltas, turned, ig = exchange(inputs, out_grad, gate_weight, up_weight, down_weight, gate_mask, up_mask, down_mask)
    deltas = deltas.reshape(3, TOK, FF)
    gate_grad, up_grad, down_grad, input_grad = grads(turned, out_grad, deltas, gate_mask, up_mask, down_mask, ig)
    return (input_grad, gate_grad, up_grad, down_grad)


def solution(mesh):
    placed = (
        P(None, "row"),
        P(None, "row"),
        P("row", "col"),
        P("row", "col"),
        P("col", "row"),
        P("row", "col"),
        P("row", "col"),
        P("col", "row"),
    )
    return jax.shard_map(
        shards,
        mesh=mesh,
        in_specs=placed,
        out_specs=(P("col", "row"), P("row", "col"), P("row", "col"), P("col", "row")),
        check_vma=False,
    )
```

```python
import jax
import jax.numpy as jnp
from jax import lax
from jax.experimental import pallas as pl
from jax.experimental.pallas import tpu as pltpu
from jax.sharding import PartitionSpec as P

MESH = pl.DeviceIdType.MESH
F32 = jnp.float32
BF16 = jnp.bfloat16
BLOCK = 128
TOK = 512
DIM = 512
FF = 1792
HALF = FF // 2
CHUNKS = 4
ROWS = 64 // CHUNKS
GROUP = 2 * ROWS
SPAN = 4 * GROUP
STEPS = 3 * CHUNKS

LAG_RING = 1
LAG_FORWARD = 3
LAG_OWN = 5
LAG_FINAL = 8
LAG_RELAY = 10
LAG_CORE = 12
LAG_GRAD = 13
LAG_COL = 15
TURN = 13

R1, R2, R3, L1, L2, L3 = range(6)


def product(left, right):
    return jnp.dot(left, right, preferred_element_type=F32)


def product_t(left, right):
    return lax.dot_general(left, right, (((1,), (1,)), ((), ())), preferred_element_type=F32)


def t_product(left, right):
    return lax.dot_general(left, right, (((0,), (0,)), ((), ())), preferred_element_type=F32)


def exchange_kernel(
    x_hbm, og_hbm, wg_hbm, wu_hbm, wd_hbm, gm_hbm, um_hbm, dm_hbm,
    d_hbm, xt_hbm, ig_out,
    gm, um, dm, x_own, og_own, xt, w_own, wd_own, core_out, core_in,
    part, send, ring, z_out, z_in, sums, deltas,
    ig, ig_x, ig_z, ig_sum, ig_in,
    local_sem, mask_sem, core_s, core_r, ring_s, ring_r, z_s, z_r, ag_s, ag_r, x_s, x_r, zl_s, zl_r,
):
    row = lax.axis_index("row")
    col = lax.axis_index("col")
    y = row // 4
    h = (row // 2) % 2
    c = row % 2
    x = col // 4
    zl = col % 4
    up = lax.rem(y + 1, 4)
    down = lax.rem(y + 3, 4)
    far = lax.rem(y + 2, 4)

    def ring_dev(yy):
        return (yy * 4 + h * 2 + c, col)

    right = ring_dev(up)
    left = ring_dev(down)
    z_dev = (y * 4 + (1 - h) * 2 + c, col)
    core_dev = (y * 4 + h * 2 + (1 - c), col)
    own_cols = pl.ds(pl.multiple_of(c * HALF, 128), HALF)
    oth_cols = pl.ds(pl.multiple_of((1 - c) * HALF, 128), HALF)

    def x_dev(d):
        return (row, lax.rem(x + d, 4) * 4 + zl)

    def remote(src, dst, ss, rs, dev):
        return pltpu.make_async_remote_copy(
            src_ref=src, dst_ref=dst, send_sem=ss, recv_sem=rs, device_id=dev, device_id_type=MESH
        )

    def chunk(k):
        return lax.rem(k + CHUNKS // 2, CHUNKS)

    def owner(k):
        return chunk(k) // (CHUNKS // 4)

    def piece(yy, hh):
        return pl.ds(pl.multiple_of(yy * GROUP + hh * ROWS, ROWS), ROWS)

    def half(hh):
        return pl.ds(pl.multiple_of(hh * ROWS, ROWS), ROWS)

    loads = [
        pltpu.make_async_copy(x_hbm, x_own, local_sem.at[0]),
        pltpu.make_async_copy(wg_hbm.at[:, oth_cols], w_own.at[0, :, oth_cols], local_sem.at[1]),
        pltpu.make_async_copy(wg_hbm.at[:, own_cols], w_own.at[0, :, own_cols], local_sem.at[5]),
        pltpu.make_async_copy(wu_hbm, w_own.at[1], local_sem.at[2]),
        pltpu.make_async_copy(og_hbm, og_own, local_sem.at[3]),
        pltpu.make_async_copy(wd_hbm, wd_own, local_sem.at[4]),
    ]
    masks = [
        pltpu.make_async_copy(gm_hbm, gm, mask_sem.at[0]),
        pltpu.make_async_copy(um_hbm, um, mask_sem.at[1]),
        pltpu.make_async_copy(dm_hbm, dm, mask_sem.at[2]),
    ]
    for load in loads[:2] + masks + loads[2:]:
        load.start()

    bar = pltpu.get_barrier_semaphore()
    friends = [right, left, z_dev, core_dev] + [x_dev(d) for d in (1, 2, 3)]
    friends += [(row, x * 4 + lax.rem(zl + d, 4)) for d in (1, 2, 3)]
    for dev in friends:
        pl.semaphore_signal(bar, inc=1, device_id=dev, device_id_type=MESH)
    pl.semaphore_wait(bar, len(friends))

    def mask_cols(which, mask_ref, first, count):
        @pl.loop(0, count * HALF // BLOCK)
        def _(n):
            j = first * (HALF // BLOCK) + n
            cols = pl.ds(pl.multiple_of(j * BLOCK, BLOCK), BLOCK)
            for i in range(DIM // BLOCK):
                rows = pl.ds(i * BLOCK, BLOCK)
                keep = jnp.full((BLOCK, BLOCK), mask_ref[i, j].astype(F32), F32).astype(BF16)
                w_own[which, rows, cols] = w_own[which, rows, cols] * keep

    def mask_rows():
        @pl.loop(0, FF // BLOCK)
        def _(j):
            rows = pl.ds(pl.multiple_of(j * BLOCK, BLOCK), BLOCK)
            for i in range(DIM // BLOCK):
                cols = pl.ds(i * BLOCK, BLOCK)
                keep = jnp.full((BLOCK, BLOCK), dm[i, j].astype(F32), F32).astype(BF16)
                wd_own[rows, cols] = wd_own[rows, cols] * keep

    def core_copy(s):
        return remote(core_out.at[s], core_in.at[s], core_s.at[s], core_r.at[s], core_dev)

    def ring_copy(kind, s, yy, hh):
        dev = right if kind in (R1, R2, R3) else left
        return remote(send.at[s, piece(yy, hh)], ring.at[kind, s], ring_s.at[kind, s], ring_r.at[kind, s], dev)

    def ring_early(s):
        return [ring_copy(R1, s, far, 0), ring_copy(L1, s, far, 1), ring_copy(R2, s, up, 1), ring_copy(L2, s, down, 0)]

    def ring_late(s):
        return [ring_copy(R3, s, up, 0), ring_copy(L3, s, down, 1)]

    def z_copy(s):
        return remote(z_out.at[s], z_in.at[s], z_s.at[s], z_r.at[s], z_dev)

    def y_copy(m, k):
        def copy(i, yy, hh, dev):
            ref = deltas.at[m, k, yy, half(hh), own_cols]
            return remote(ref, ref, ag_s.at[m, k, i], ag_r.at[m, k, i], dev)

        return copy

    def pair_copy(m, k, cols):
        ref = deltas.at[m, k, :, :, cols]
        return remote(ref, ref, ag_s.at[m, k, 6], ag_r.at[m, k, 6], core_dev)

    def gather_own(*copies):
        for copy in copies:
            copy(0, y, 0, right).start()
            copy(3, y, 1, left).start()
        for copy in copies:
            copy(1, y, 1, right).start()
            copy(2, y, 0, left).start()

    def gather_relay(copy):
        copy(0, down, 0, right).wait_recv()
        copy(4, down, 0, right).start()
        copy(3, up, 1, left).wait_recv()
        copy(5, up, 1, left).start()

    def gather_rest(copy):
        copy(1, down, 1, right).wait_recv()
        copy(2, up, 0, left).wait_recv()
        copy(4, far, 0, right).wait_recv()
        copy(5, far, 1, left).wait_recv()

    def gather_drain(copy):
        for hh in range(2):
            copy(hh, y, hh, right).wait_send()
            copy(2 + hh, y, hh, left).wait_send()
        copy(4, down, 0, right).wait_send()
        copy(5, up, 1, left).wait_send()

    def out_copy(k):
        return pltpu.make_async_copy(
            deltas.at[pl.ds(1, 2), k], d_hbm.at[pl.ds(1, 2), :, chunk(k)], local_sem.at[7 + k]
        )

    def hidden_store(k):
        return pltpu.make_async_copy(deltas.at[0, k], d_hbm.at[0, :, chunk(k)], local_sem.at[7 + CHUNKS + k])

    xt_copy = pltpu.make_async_copy(xt, xt_hbm, local_sem.at[6])

    def x_copy(k, d):
        return remote(
            ig.at[k, lax.rem(x + d, 4)], ig_x.at[k, d - 1], x_s.at[k, d - 1], x_r.at[k, d - 1], x_dev(d)
        )

    def zl_copy(k):
        slot = lax.rem(zl - owner(k) + 7, 4)
        part_of = lax.rem(chunk(k), CHUNKS // 4)
        return remote(
            ig_z.at[k], ig_in.at[part_of, slot], zl_s.at[k], zl_r.at[part_of, slot], (row, x * 4 + owner(k))
        )

    def reduce_col(k):
        total = ig[k, x]
        for d in (1, 2, 3):
            x_copy(k, d).wait_recv()
            total = total + ig_x[k, d - 1]

        @pl.when(zl == owner(k))
        def _():
            ig_sum[lax.rem(chunk(k), CHUNKS // 4)] = total

        @pl.when(zl != owner(k))
        def _():
            ig_z[k] = total.astype(BF16)
            zl_copy(k).start()

    def drain(k):
        for m in range(3):
            gather_drain(y_copy(m, k))
            pair_copy(m, k, own_cols).wait_send()
        for d in (1, 2, 3):
            x_copy(k, d).wait_send()

        @pl.when(zl != owner(k))
        def _():
            zl_copy(k).wait_send()

        out_copy(k).wait()
        hidden_store(k).wait()

    def at_chunk(s, lag, fn, count=CHUNKS):
        @pl.when((s >= lag + 2) & (s < 3 * count + lag) & (lax.rem(s + 3 * 32 - lag, 3) == 2))
        def _():
            fn((s - lag) // 3)

    @pl.loop(0, STEPS + LAG_COL)
    def _(s):
        @pl.when(s < STEPS)
        def _():
            m = lax.rem(s, 3)
            t = chunk(s // 3)

            @pl.when(s == 0)
            def _():
                loads[0].wait()
                loads[1].wait()
                masks[0].wait()
                mask_cols(0, gm, 1 - c, 1)

            @pl.when(s == 1)
            def _():
                loads[3].wait()
                masks[1].wait()
                mask_cols(1, um, 0, 2)

            @pl.when(s == 2)
            def _():
                loads[4].wait()
                loads[5].wait()
                masks[2].wait()
                mask_rows()

            @pl.when(m < 2)
            def _():
                rows = x_own[:, t].reshape(SPAN, DIM)
                core_out[s] = product(rows, w_own[m, :, oth_cols])
                core_copy(s).start()

                @pl.when(s == 0)
                def _():
                    loads[2].wait()
                    mask_cols(0, gm, c, 1)

                part[s] = product(rows, w_own[m, :, own_cols])

            @pl.when(m == 2)
            def _():
                rows = og_own[:, t].reshape(SPAN, DIM)
                core_out[s] = product_t(rows, wd_own[oth_cols, :])
                core_copy(s).start()
                part[s] = product_t(rows, wd_own[own_cols, :])

        @pl.when((s >= LAG_RING) & (s < STEPS + LAG_RING))
        def _():
            n = s - LAG_RING
            core_copy(n).wait_recv()
            value = part[n] + core_in[n]
            part[n] = value
            send[n] = value.astype(BF16)
            for copy in ring_early(n):
                copy.start()

        @pl.when((s >= LAG_FORWARD) & (s < STEPS + LAG_FORWARD))
        def _():
            n = s - LAG_FORWARD
            first = ring_early(n)[:2]
            onward = ring_late(n)
            first[0].wait_recv()
            send[n, piece(up, 0)] = (part[n, piece(up, 0)] + ring[R1, n].astype(F32)).astype(BF16)
            onward[0].start()
            first[1].wait_recv()
            send[n, piece(down, 1)] = (part[n, piece(down, 1)] + ring[L1, n].astype(F32)).astype(BF16)
            onward[1].start()

        @pl.when((s >= LAG_OWN) & (s < STEPS + LAG_OWN))
        def _():
            n = s - LAG_OWN
            for copy in ring_early(n)[2:] + ring_late(n):
                copy.wait_recv()
            first = part[n, piece(y, 0)] + ring[R3, n].astype(F32) + ring[L2, n].astype(F32)
            second = part[n, piece(y, 1)] + ring[L3, n].astype(F32) + ring[R2, n].astype(F32)
            sums[n, 0:ROWS] = first
            sums[n, ROWS : 2 * ROWS] = second
            z_out[n, 0:ROWS] = first.astype(BF16)
            z_out[n, ROWS : 2 * ROWS] = second.astype(BF16)
            z_copy(n).start()

        @pl.when((s >= LAG_FINAL) & (s < STEPS + LAG_FINAL))
        def _():
            n = s - LAG_FINAL
            z_copy(n).wait_recv()
            sums[n] = sums[n] + z_in[n].astype(F32)
            core_copy(n).wait_send()
            for copy in ring_early(n) + ring_late(n):
                copy.wait_send()
            z_copy(n).wait_send()

        @pl.when(s == TURN)
        def _():
            xt[...] = x_own[...].reshape(TOK, DIM).T
            xt_copy.start()

        def pointwise(k):
            gate = sums[3 * k]
            upv = sums[3 * k + 1]
            back = sums[3 * k + 2]
            sig = jax.nn.sigmoid(gate)
            slope = sig * (1.0 + gate * (1.0 - sig))
            deltas[1, k, y, :, own_cols] = (back * upv * slope).astype(BF16)
            deltas[2, k, y, :, own_cols] = (back * gate * sig).astype(BF16)
            gather_own(y_copy(1, k), y_copy(2, k))
            deltas[0, k, y, :, own_cols] = (gate * sig * upv).astype(BF16)

        def relay(k):
            gather_relay(y_copy(1, k))
            gather_relay(y_copy(2, k))
            gather_own(y_copy(0, k))

        def to_core(k):
            for m in (1, 2):
                gather_rest(y_copy(m, k))
                pair_copy(m, k, own_cols).start()
            gather_relay(y_copy(0, k))

        def grad(k):
            pair_copy(1, k, oth_cols).wait_recv()
            value = product_t(deltas[1, k].reshape(SPAN, FF), w_own[0])
            pair_copy(2, k, oth_cols).wait_recv()
            value = value + product_t(deltas[2, k].reshape(SPAN, FF), w_own[1])
            ig[k] = value.reshape(4, GROUP, DIM)
            for d in (2, 1, 3):
                x_copy(k, d).start()
            out_copy(k).start()
            gather_rest(y_copy(0, k))
            pair_copy(0, k, own_cols).start()

        def finish(k):
            pair_copy(0, k, oth_cols).wait_recv()
            hidden_store(k).start()
            reduce_col(k)

            @pl.when(k > 0)
            def _():
                drain(k - 1)

        at_chunk(s, LAG_FINAL, pointwise)
        at_chunk(s, LAG_RELAY, relay)
        at_chunk(s, LAG_CORE, to_core)
        at_chunk(s, LAG_GRAD, grad)
        at_chunk(s, LAG_COL, finish)

    for part_of in range(CHUNKS // 4):
        total = ig_sum[part_of]
        for i in range(3):
            remote(
                ig_z.at[0], ig_in.at[part_of, i], zl_s.at[0], zl_r.at[part_of, i], core_dev
            ).wait_recv()
            total = total + ig_in[part_of, i].astype(F32)
        ig_out[pl.ds(part_of * GROUP, GROUP)] = total.astype(BF16)

    drain(CHUNKS - 1)
    xt_copy.wait()


def exchange(inputs, out_grad, gate_weight, up_weight, down_weight, gate_mask, up_mask, down_mask):
    any_spec = pl.BlockSpec(memory_space=pl.ANY)
    small = pltpu.SMEM((DIM // BLOCK, FF // BLOCK), jnp.int32)
    dma = pltpu.SemaphoreType.DMA
    return pl.pallas_call(
        exchange_kernel,
        out_shape=(
            jax.ShapeDtypeStruct((3, 4, CHUNKS, GROUP, FF), BF16),
            jax.ShapeDtypeStruct((DIM, TOK), BF16),
            jax.ShapeDtypeStruct((32, DIM), BF16),
        ),
        in_specs=[any_spec] * 8,
        out_specs=(any_spec, any_spec, pl.BlockSpec(memory_space=pltpu.VMEM)),
        scratch_shapes=[
            small,
            small,
            small,
            pltpu.VMEM((4, CHUNKS, GROUP, DIM), BF16),
            pltpu.VMEM((4, CHUNKS, GROUP, DIM), BF16),
            pltpu.VMEM((DIM, TOK), BF16),
            pltpu.VMEM((2, DIM, FF), BF16),
            pltpu.VMEM((FF, DIM), BF16),
            pltpu.VMEM((STEPS, SPAN, HALF), F32),
            pltpu.VMEM((STEPS, SPAN, HALF), F32),
            pltpu.VMEM((STEPS, SPAN, HALF), F32),
            pltpu.VMEM((STEPS, SPAN, HALF), BF16),
            pltpu.VMEM((6, STEPS, ROWS, HALF), BF16),
            pltpu.VMEM((STEPS, 2 * ROWS, HALF), BF16),
            pltpu.VMEM((STEPS, 2 * ROWS, HALF), BF16),
            pltpu.VMEM((STEPS, 2 * ROWS, HALF), F32),
            pltpu.VMEM((3, CHUNKS, 4, GROUP, FF), BF16),
            pltpu.VMEM((CHUNKS, 4, GROUP, DIM), F32),
            pltpu.VMEM((CHUNKS, 3, GROUP, DIM), F32),
            pltpu.VMEM((CHUNKS, GROUP, DIM), BF16),
            pltpu.VMEM((CHUNKS // 4, GROUP, DIM), F32),
            pltpu.VMEM((CHUNKS // 4, 3, GROUP, DIM), BF16),
            dma((7 + 2 * CHUNKS,)),
            dma((3,)),
            dma((STEPS,)),
            dma((STEPS,)),
            dma((6, STEPS)),
            dma((6, STEPS)),
            dma((STEPS,)),
            dma((STEPS,)),
            dma((3, CHUNKS, 7)),
            dma((3, CHUNKS, 7)),
            dma((CHUNKS, 3)),
            dma((CHUNKS, 3)),
            dma((CHUNKS,)),
            dma((CHUNKS // 4, 3)),
        ],
        compiler_params=pltpu.CompilerParams(
            collective_id=0, has_side_effects=True, vmem_limit_bytes=58 * 2**20
        ),
        name="exchange",
    )(
        inputs.reshape(4, CHUNKS, GROUP, DIM),
        out_grad.reshape(4, CHUNKS, GROUP, DIM),
        gate_weight,
        up_weight,
        down_weight,
        gate_mask,
        up_mask,
        down_mask.T,
    )


def grads_kernel(
    xt_hbm, og_hbm, d_hbm, gm_hbm, um_hbm, dm_hbm, ig_hbm,
    gate_hbm, up_hbm, down_hbm, ig_out_hbm,
    gm, um, dm, ig, xt, og, d, cols_out, rows_out, sem_in, sem_out,
):
    head = pl.ds(0, 768)
    tail = pl.ds(768, FF - 768)
    loads = [
        pltpu.make_async_copy(xt_hbm, xt, sem_in.at[0]),
        pltpu.make_async_copy(d_hbm.at[1, :, head], d.at[1, :, head], sem_in.at[1]),
        pltpu.make_async_copy(gm_hbm, gm, sem_in.at[2]),
        pltpu.make_async_copy(d_hbm.at[1, :, tail], d.at[1, :, tail], sem_in.at[3]),
        pltpu.make_async_copy(um_hbm, um, sem_in.at[4]),
        pltpu.make_async_copy(d_hbm.at[2], d.at[2], sem_in.at[5]),
        pltpu.make_async_copy(dm_hbm, dm, sem_in.at[6]),
        pltpu.make_async_copy(ig_hbm, ig, sem_in.at[7]),
        pltpu.make_async_copy(og_hbm, og, sem_in.at[8]),
        pltpu.make_async_copy(d_hbm.at[0], d.at[0], sem_in.at[9]),
    ]
    for load in loads:
        load.start()
    for load in loads[:3]:
        load.wait()
    ig_store = pltpu.make_async_copy(ig, ig_out_hbm, sem_out.at[2 + FF // 256])
    stores = [
        pltpu.make_async_copy(cols_out.at[0], gate_hbm, sem_out.at[0]),
        pltpu.make_async_copy(cols_out.at[1], up_hbm, sem_out.at[1]),
    ]
    for which, mask in ((1, gm), (2, um)):
        if which == 2:
            loads[4].wait()
            loads[5].wait()
        for j in range(FF // 256):
            if which == 1 and j == 3:
                loads[3].wait()
            value = product(xt[...], d[which, :, j * 256 : (j + 1) * 256])
            for k in range(2):
                cols = pl.ds(j * 256 + k * BLOCK, BLOCK)
                for i in range(DIM // BLOCK):
                    rows = slice(i * BLOCK, (i + 1) * BLOCK)
                    keep = mask[i, 2 * j + k].astype(F32)
                    part = value[rows, k * BLOCK : (k + 1) * BLOCK] * keep
                    cols_out[which - 1, rows, cols] = part.astype(BF16)

        stores[which - 1].start()
    for load in loads[6:]:
        load.wait()
    ig_store.start()

    def store_rows(j):
        rows = pl.ds(j * 256, 256)
        return pltpu.make_async_copy(rows_out.at[rows], down_hbm.at[rows], sem_out.at[2 + j])

    for j in range(FF // 256):
        value = t_product(d[0, :, j * 256 : (j + 1) * 256], og[...])
        for k in range(2):
            rows = pl.ds(j * 256 + k * BLOCK, BLOCK)
            for i in range(DIM // BLOCK):
                cols = slice(i * BLOCK, (i + 1) * BLOCK)
                keep = dm[i, 2 * j + k].astype(F32)
                part = value[k * BLOCK : (k + 1) * BLOCK, cols] * keep
                rows_out[rows, cols] = part.astype(BF16)
        store_rows(j).start()

    ig_store.wait()
    for store in stores:
        store.wait()
    for j in range(FF // 256):
        store_rows(j).wait()


def grads(turned, out_grad, deltas, gate_mask, up_mask, down_mask, ig):
    any_spec = pl.BlockSpec(memory_space=pl.ANY)
    small = pltpu.SMEM((DIM // BLOCK, FF // BLOCK), jnp.int32)
    return pl.pallas_call(
        grads_kernel,
        out_shape=(
            jax.ShapeDtypeStruct((DIM, FF), BF16),
            jax.ShapeDtypeStruct((DIM, FF), BF16),
            jax.ShapeDtypeStruct((FF, DIM), BF16),
            jax.ShapeDtypeStruct((32, DIM), BF16),
        ),
        in_specs=[any_spec] * 7,
        out_specs=(any_spec,) * 4,
        scratch_shapes=[
            small,
            small,
            small,
            pltpu.VMEM((32, DIM), BF16),
            pltpu.VMEM((DIM, TOK), BF16),
            pltpu.VMEM((TOK, DIM), BF16),
            pltpu.VMEM((3, TOK, FF), BF16),
            pltpu.VMEM((2, DIM, FF), BF16),
            pltpu.VMEM((FF, DIM), BF16),
            pltpu.SemaphoreType.DMA((10,)),
            pltpu.SemaphoreType.DMA((3 + FF // 256,)),
        ],
        compiler_params=pltpu.CompilerParams(vmem_limit_bytes=62 * 2**20),
        name="grads",
    )(turned, out_grad, deltas, gate_mask, up_mask, down_mask.T, ig)


def shards(inputs, out_grad, gate_weight, up_weight, down_weight, gate_mask, up_mask, down_mask):
    deltas, turned, ig = exchange(inputs, out_grad, gate_weight, up_weight, down_weight, gate_mask, up_mask, down_mask)
    deltas = deltas.reshape(3, TOK, FF)
    gate_grad, up_grad, down_grad, input_grad = grads(turned, out_grad, deltas, gate_mask, up_mask, down_mask, ig)
    return (input_grad, gate_grad, up_grad, down_grad)


def solution(mesh):
    placed = (
        P(None, "row"),
        P(None, "row"),
        P("row", "col"),
        P("row", "col"),
        P("col", "row"),
        P("row", "col"),
        P("row", "col"),
        P("col", "row"),
    )
    return jax.shard_map(
        shards,
        mesh=mesh,
        in_specs=placed,
        out_specs=(P("col", "row"), P("row", "col"), P("row", "col"), P("col", "row")),
        check_vma=False,
    )
```

```python
import jax
import jax.numpy as jnp
from jax import lax
from jax.experimental import pallas as pl
from jax.experimental.pallas import tpu as pltpu
from jax.sharding import PartitionSpec as P

MESH = pl.DeviceIdType.MESH
F32 = jnp.float32
BF16 = jnp.bfloat16
BLOCK = 128
TOK = 512
DIM = 512
FF = 1792
HALF = FF // 2
CHUNKS = 4
ROWS = 64 // CHUNKS
GROUP = 2 * ROWS
SPAN = 4 * GROUP
PARTS = 1
STEPS = 3 * CHUNKS

LAG_RING = 1
LAG_FORWARD = 3
LAG_OWN = 5
LAG_FINAL = 8
LAG_RELAY = 10
LAG_CORE = 12
LAG_GRAD = 13
LAG_COL = 15
TURN = 13

R1, R2, R3, L1, L2, L3 = range(6)


def product(left, right):
    return jnp.dot(left, right, preferred_element_type=F32)


def product_t(left, right):
    return lax.dot_general(left, right, (((1,), (1,)), ((), ())), preferred_element_type=F32)


def t_product(left, right):
    return lax.dot_general(left, right, (((0,), (0,)), ((), ())), preferred_element_type=F32)


def exchange_kernel(
    x_hbm, og_hbm, wg_hbm, wu_hbm, wd_hbm, gm_hbm, um_hbm, dm_hbm,
    d_hbm, xt_hbm, ig_out,
    gm, um, dm, x_own, og_own, xt, w_own, wd_own, core_out, core_in,
    part, send, ring, z_out, z_in, sums, deltas,
    ig, ig_x, ig_z, ig_sum, ig_in,
    local_sem, mask_sem, core_s, core_r, ring_s, ring_r, z_s, z_r, ag_s, ag_r, x_s, x_r, zl_s, zl_r,
):
    row = lax.axis_index("row")
    col = lax.axis_index("col")
    y = row // 4
    h = (row // 2) % 2
    c = row % 2
    x = col // 4
    zl = col % 4
    up = lax.rem(y + 1, 4)
    down = lax.rem(y + 3, 4)
    far = lax.rem(y + 2, 4)

    def ring_dev(yy):
        return (yy * 4 + h * 2 + c, col)

    right = ring_dev(up)
    left = ring_dev(down)
    z_dev = (y * 4 + (1 - h) * 2 + c, col)
    core_dev = (y * 4 + h * 2 + (1 - c), col)
    own_cols = pl.ds(pl.multiple_of(c * HALF, 128), HALF)
    oth_cols = pl.ds(pl.multiple_of((1 - c) * HALF, 128), HALF)

    def x_dev(d):
        return (row, lax.rem(x + d, 4) * 4 + zl)

    def remote(src, dst, ss, rs, dev):
        return pltpu.make_async_remote_copy(
            src_ref=src, dst_ref=dst, send_sem=ss, recv_sem=rs, device_id=dev, device_id_type=MESH
        )

    def chunk(k):
        return lax.rem(k + CHUNKS // 2, CHUNKS)

    def owner(k):
        return chunk(k) // (CHUNKS // 4)

    def piece(yy, hh):
        return pl.ds(pl.multiple_of(yy * GROUP + hh * ROWS, ROWS), ROWS)

    def half(hh):
        return pl.ds(pl.multiple_of(hh * ROWS, ROWS), ROWS)

    loads = [
        pltpu.make_async_copy(x_hbm, x_own, local_sem.at[0]),
        pltpu.make_async_copy(wg_hbm.at[:, oth_cols], w_own.at[0, :, oth_cols], local_sem.at[1]),
        pltpu.make_async_copy(wg_hbm.at[:, own_cols], w_own.at[0, :, own_cols], local_sem.at[5]),
        pltpu.make_async_copy(wu_hbm, w_own.at[1], local_sem.at[2]),
        pltpu.make_async_copy(og_hbm, og_own, local_sem.at[3]),
        pltpu.make_async_copy(wd_hbm, wd_own, local_sem.at[4]),
    ]
    masks = [
        pltpu.make_async_copy(gm_hbm, gm, mask_sem.at[0]),
        pltpu.make_async_copy(um_hbm, um, mask_sem.at[1]),
        pltpu.make_async_copy(dm_hbm, dm, mask_sem.at[2]),
    ]
    for load in loads[:2] + masks + loads[2:]:
        load.start()

    bar = pltpu.get_barrier_semaphore()
    friends = [right, left, z_dev, core_dev] + [x_dev(d) for d in (1, 2, 3)]
    friends += [(row, x * 4 + lax.rem(zl + d, 4)) for d in (1, 2, 3)]
    for dev in friends:
        pl.semaphore_signal(bar, inc=1, device_id=dev, device_id_type=MESH)
    pl.semaphore_wait(bar, len(friends))

    def mask_cols(which, mask_ref, first, count):
        @pl.loop(0, count * HALF // BLOCK)
        def _(n):
            j = first * (HALF // BLOCK) + n
            cols = pl.ds(pl.multiple_of(j * BLOCK, BLOCK), BLOCK)
            for i in range(DIM // BLOCK):
                rows = pl.ds(i * BLOCK, BLOCK)
                keep = jnp.full((BLOCK, BLOCK), mask_ref[i, j].astype(F32), F32).astype(BF16)
                w_own[which, rows, cols] = w_own[which, rows, cols] * keep

    def mask_rows():
        @pl.loop(0, FF // BLOCK)
        def _(j):
            rows = pl.ds(pl.multiple_of(j * BLOCK, BLOCK), BLOCK)
            for i in range(DIM // BLOCK):
                cols = pl.ds(i * BLOCK, BLOCK)
                keep = jnp.full((BLOCK, BLOCK), dm[i, j].astype(F32), F32).astype(BF16)
                wd_own[rows, cols] = wd_own[rows, cols] * keep

    def core_copy(s):
        return remote(core_out.at[s], core_in.at[s], core_s.at[s], core_r.at[s], core_dev)

    def ring_copy(kind, s, yy, hh):
        dev = right if kind in (R1, R2, R3) else left
        return remote(send.at[s, piece(yy, hh)], ring.at[kind, s], ring_s.at[kind, s], ring_r.at[kind, s], dev)

    def ring_early(s):
        return [ring_copy(R1, s, far, 0), ring_copy(L1, s, far, 1), ring_copy(R2, s, up, 1), ring_copy(L2, s, down, 0)]

    def ring_late(s):
        return [ring_copy(R3, s, up, 0), ring_copy(L3, s, down, 1)]

    def z_copy(s):
        return remote(z_out.at[s], z_in.at[s], z_s.at[s], z_r.at[s], z_dev)

    def y_copy(m, k):
        def copy(i, yy, hh, dev):
            ref = deltas.at[m, k, yy, half(hh), own_cols]
            return remote(ref, ref, ag_s.at[m, k, i], ag_r.at[m, k, i], dev)

        return copy

    def pair_copy(m, k, cols):
        ref = deltas.at[m, k, :, :, cols]
        return remote(ref, ref, ag_s.at[m, k, 6], ag_r.at[m, k, 6], core_dev)

    def gather_own(*copies):
        for copy in copies:
            copy(0, y, 0, right).start()
            copy(3, y, 1, left).start()
        for copy in copies:
            copy(1, y, 1, right).start()
            copy(2, y, 0, left).start()

    def gather_relay(copy):
        copy(0, down, 0, right).wait_recv()
        copy(4, down, 0, right).start()
        copy(3, up, 1, left).wait_recv()
        copy(5, up, 1, left).start()

    def gather_rest(copy):
        copy(1, down, 1, right).wait_recv()
        copy(2, up, 0, left).wait_recv()
        copy(4, far, 0, right).wait_recv()
        copy(5, far, 1, left).wait_recv()

    def gather_drain(copy):
        for hh in range(2):
            copy(hh, y, hh, right).wait_send()
            copy(2 + hh, y, hh, left).wait_send()
        copy(4, down, 0, right).wait_send()
        copy(5, up, 1, left).wait_send()

    def out_copy(k):
        return pltpu.make_async_copy(
            deltas.at[pl.ds(1, 2), k], d_hbm.at[pl.ds(1, 2), :, chunk(k)], local_sem.at[7 + k]
        )

    def hidden_store(k):
        return pltpu.make_async_copy(deltas.at[0, k], d_hbm.at[0, :, chunk(k)], local_sem.at[7 + CHUNKS + k])

    xt_copy = pltpu.make_async_copy(xt, xt_hbm, local_sem.at[6])

    def span(part):
        return pl.ds(part * (DIM // PARTS), DIM // PARTS)

    def x_copy(k, d, part):
        return remote(
            ig.at[k, lax.rem(x + d, 4), :, span(part)],
            ig_x.at[k, d - 1, :, span(part)],
            x_s.at[k, d - 1, part],
            x_r.at[k, d - 1, part],
            x_dev(d),
        )

    def zl_copy(k, part):
        slot = lax.rem(zl - owner(k) + 7, 4)
        part_of = lax.rem(chunk(k), CHUNKS // 4)
        return remote(
            ig_z.at[k, :, span(part)],
            ig_in.at[part_of, slot, :, span(part)],
            zl_s.at[k, part],
            zl_r.at[part_of, slot, part],
            (row, x * 4 + owner(k)),
        )

    def reduce_col(k):
        for part in range(PARTS):
            total = ig[k, x, :, span(part)]
            for d in (1, 2, 3):
                x_copy(k, d, part).wait_recv()
                total = total + ig_x[k, d - 1, :, span(part)]

            @pl.when(zl == owner(k))
            def _():
                ig_sum[lax.rem(chunk(k), CHUNKS // 4), :, span(part)] = total

            @pl.when(zl != owner(k))
            def _():
                ig_z[k, :, span(part)] = total.astype(BF16)
                zl_copy(k, part).start()

    def drain(k):
        for m in range(3):
            gather_drain(y_copy(m, k))
            pair_copy(m, k, own_cols).wait_send()
        for part in range(PARTS):
            for d in (1, 2, 3):
                x_copy(k, d, part).wait_send()

        @pl.when(zl != owner(k))
        def _():
            for part in range(PARTS):
                zl_copy(k, part).wait_send()

        out_copy(k).wait()
        hidden_store(k).wait()

    def at_chunk(s, lag, fn, count=CHUNKS):
        @pl.when((s >= lag + 2) & (s < 3 * count + lag) & (lax.rem(s + 3 * 32 - lag, 3) == 2))
        def _():
            fn((s - lag) // 3)

    @pl.loop(0, STEPS + LAG_COL)
    def _(s):
        @pl.when(s < STEPS)
        def _():
            m = lax.rem(s, 3)
            t = chunk(s // 3)

            @pl.when(s == 0)
            def _():
                loads[0].wait()
                loads[1].wait()
                masks[0].wait()
                mask_cols(0, gm, 1 - c, 1)

            @pl.when(s == 1)
            def _():
                loads[3].wait()
                masks[1].wait()
                mask_cols(1, um, 0, 2)

            @pl.when(s == 2)
            def _():
                loads[4].wait()
                loads[5].wait()
                masks[2].wait()
                mask_rows()

            @pl.when(m < 2)
            def _():
                rows = x_own[:, t].reshape(SPAN, DIM)
                core_out[s] = product(rows, w_own[m, :, oth_cols])
                core_copy(s).start()

                @pl.when(s == 0)
                def _():
                    loads[2].wait()
                    mask_cols(0, gm, c, 1)

                part[s] = product(rows, w_own[m, :, own_cols])

            @pl.when(m == 2)
            def _():
                rows = og_own[:, t].reshape(SPAN, DIM)
                core_out[s] = product_t(rows, wd_own[oth_cols, :])
                core_copy(s).start()
                part[s] = product_t(rows, wd_own[own_cols, :])

        @pl.when((s >= LAG_RING) & (s < STEPS + LAG_RING))
        def _():
            n = s - LAG_RING
            core_copy(n).wait_recv()
            value = part[n] + core_in[n]
            part[n] = value
            send[n] = value.astype(BF16)
            for copy in ring_early(n):
                copy.start()

        @pl.when((s >= LAG_FORWARD) & (s < STEPS + LAG_FORWARD))
        def _():
            n = s - LAG_FORWARD
            first = ring_early(n)[:2]
            onward = ring_late(n)
            first[0].wait_recv()
            send[n, piece(up, 0)] = (part[n, piece(up, 0)] + ring[R1, n].astype(F32)).astype(BF16)
            onward[0].start()
            first[1].wait_recv()
            send[n, piece(down, 1)] = (part[n, piece(down, 1)] + ring[L1, n].astype(F32)).astype(BF16)
            onward[1].start()

        @pl.when((s >= LAG_OWN) & (s < STEPS + LAG_OWN))
        def _():
            n = s - LAG_OWN
            for copy in ring_early(n)[2:] + ring_late(n):
                copy.wait_recv()
            first = part[n, piece(y, 0)] + ring[R3, n].astype(F32) + ring[L2, n].astype(F32)
            second = part[n, piece(y, 1)] + ring[L3, n].astype(F32) + ring[R2, n].astype(F32)
            sums[n, 0:ROWS] = first
            sums[n, ROWS : 2 * ROWS] = second
            z_out[n, 0:ROWS] = first.astype(BF16)
            z_out[n, ROWS : 2 * ROWS] = second.astype(BF16)
            z_copy(n).start()

        @pl.when((s >= LAG_FINAL) & (s < STEPS + LAG_FINAL))
        def _():
            n = s - LAG_FINAL
            z_copy(n).wait_recv()
            sums[n] = sums[n] + z_in[n].astype(F32)
            core_copy(n).wait_send()
            for copy in ring_early(n) + ring_late(n):
                copy.wait_send()
            z_copy(n).wait_send()

        @pl.when(s == TURN)
        def _():
            xt[...] = x_own[...].reshape(TOK, DIM).T
            xt_copy.start()

        def pointwise(k):
            gate = sums[3 * k]
            upv = sums[3 * k + 1]
            back = sums[3 * k + 2]
            sig = jax.nn.sigmoid(gate)
            slope = sig * (1.0 + gate * (1.0 - sig))
            deltas[1, k, y, :, own_cols] = (back * upv * slope).astype(BF16)
            deltas[2, k, y, :, own_cols] = (back * gate * sig).astype(BF16)
            gather_own(y_copy(1, k), y_copy(2, k))
            deltas[0, k, y, :, own_cols] = (gate * sig * upv).astype(BF16)

        def relay(k):
            gather_relay(y_copy(1, k))
            gather_relay(y_copy(2, k))
            gather_own(y_copy(0, k))

        def hidden_half(k, cols, rows):
            return product_t(deltas[1, k, :, :, cols].reshape(SPAN, HALF), w_own[0, rows, cols]) + product_t(
                deltas[2, k, :, :, cols].reshape(SPAN, HALF), w_own[1, rows, cols]
            )

        def to_core(k):
            for m in (1, 2):
                gather_rest(y_copy(m, k))
                pair_copy(m, k, own_cols).start()
            ig[k] = hidden_half(k, own_cols, pl.ds(0, DIM)).reshape(4, GROUP, DIM)
            gather_relay(y_copy(0, k))

        def grad(k):
            pair_copy(1, k, oth_cols).wait_recv()
            pair_copy(2, k, oth_cols).wait_recv()
            for part in range(PARTS):
                value = hidden_half(k, oth_cols, span(part)).reshape(4, GROUP, DIM // PARTS)
                ig[k, :, :, span(part)] = ig[k, :, :, span(part)] + value
                for d in (2, 1, 3):
                    x_copy(k, d, part).start()
            out_copy(k).start()
            gather_rest(y_copy(0, k))
            pair_copy(0, k, own_cols).start()

        def finish(k):
            pair_copy(0, k, oth_cols).wait_recv()
            hidden_store(k).start()
            reduce_col(k)

            @pl.when(k > 0)
            def _():
                drain(k - 1)

        at_chunk(s, LAG_FINAL, pointwise)
        at_chunk(s, LAG_RELAY, relay)
        at_chunk(s, LAG_CORE, to_core)
        at_chunk(s, LAG_GRAD, grad)
        at_chunk(s, LAG_COL, finish)

    for part_of in range(CHUNKS // 4):
        for part in range(PARTS):
            total = ig_sum[part_of, :, span(part)]
            for i in range(3):
                remote(
                    ig_z.at[0, :, span(part)],
                    ig_in.at[part_of, i, :, span(part)],
                    zl_s.at[0, part],
                    zl_r.at[part_of, i, part],
                    core_dev,
                ).wait_recv()
                total = total + ig_in[part_of, i, :, span(part)].astype(F32)
            ig_out[pl.ds(part_of * GROUP, GROUP), span(part)] = total.astype(BF16)

    drain(CHUNKS - 1)
    xt_copy.wait()


def exchange(inputs, out_grad, gate_weight, up_weight, down_weight, gate_mask, up_mask, down_mask):
    any_spec = pl.BlockSpec(memory_space=pl.ANY)
    small = pltpu.SMEM((DIM // BLOCK, FF // BLOCK), jnp.int32)
    dma = pltpu.SemaphoreType.DMA
    return pl.pallas_call(
        exchange_kernel,
        out_shape=(
            jax.ShapeDtypeStruct((3, 4, CHUNKS, GROUP, FF), BF16),
            jax.ShapeDtypeStruct((DIM, TOK), BF16),
            jax.ShapeDtypeStruct((32, DIM), BF16),
        ),
        in_specs=[any_spec] * 8,
        out_specs=(any_spec, any_spec, pl.BlockSpec(memory_space=pltpu.VMEM)),
        scratch_shapes=[
            small,
            small,
            small,
            pltpu.VMEM((4, CHUNKS, GROUP, DIM), BF16),
            pltpu.VMEM((4, CHUNKS, GROUP, DIM), BF16),
            pltpu.VMEM((DIM, TOK), BF16),
            pltpu.VMEM((2, DIM, FF), BF16),
            pltpu.VMEM((FF, DIM), BF16),
            pltpu.VMEM((STEPS, SPAN, HALF), F32),
            pltpu.VMEM((STEPS, SPAN, HALF), F32),
            pltpu.VMEM((STEPS, SPAN, HALF), F32),
            pltpu.VMEM((STEPS, SPAN, HALF), BF16),
            pltpu.VMEM((6, STEPS, ROWS, HALF), BF16),
            pltpu.VMEM((STEPS, 2 * ROWS, HALF), BF16),
            pltpu.VMEM((STEPS, 2 * ROWS, HALF), BF16),
            pltpu.VMEM((STEPS, 2 * ROWS, HALF), F32),
            pltpu.VMEM((3, CHUNKS, 4, GROUP, FF), BF16),
            pltpu.VMEM((CHUNKS, 4, GROUP, DIM), F32),
            pltpu.VMEM((CHUNKS, 3, GROUP, DIM), F32),
            pltpu.VMEM((CHUNKS, GROUP, DIM), BF16),
            pltpu.VMEM((CHUNKS // 4, GROUP, DIM), F32),
            pltpu.VMEM((CHUNKS // 4, 3, GROUP, DIM), BF16),
            dma((7 + 2 * CHUNKS,)),
            dma((3,)),
            dma((STEPS,)),
            dma((STEPS,)),
            dma((6, STEPS)),
            dma((6, STEPS)),
            dma((STEPS,)),
            dma((STEPS,)),
            dma((3, CHUNKS, 7)),
            dma((3, CHUNKS, 7)),
            dma((CHUNKS, 3, PARTS)),
            dma((CHUNKS, 3, PARTS)),
            dma((CHUNKS, PARTS)),
            dma((CHUNKS // 4, 3, PARTS)),
        ],
        compiler_params=pltpu.CompilerParams(
            collective_id=0, has_side_effects=True, vmem_limit_bytes=58 * 2**20
        ),
        name="exchange",
    )(
        inputs.reshape(4, CHUNKS, GROUP, DIM),
        out_grad.reshape(4, CHUNKS, GROUP, DIM),
        gate_weight,
        up_weight,
        down_weight,
        gate_mask,
        up_mask,
        down_mask.T,
    )


def grads_kernel(
    xt_hbm, og_hbm, d_hbm, gm_hbm, um_hbm, dm_hbm, ig_hbm,
    gate_hbm, up_hbm, down_hbm, ig_out_hbm,
    gm, um, dm, ig, xt, og, d, cols_out, rows_out, sem_in, sem_out,
):
    head = pl.ds(0, 768)
    tail = pl.ds(768, FF - 768)
    loads = [
        pltpu.make_async_copy(xt_hbm, xt, sem_in.at[0]),
        pltpu.make_async_copy(d_hbm.at[1, :, head], d.at[1, :, head], sem_in.at[1]),
        pltpu.make_async_copy(gm_hbm, gm, sem_in.at[2]),
        pltpu.make_async_copy(d_hbm.at[1, :, tail], d.at[1, :, tail], sem_in.at[3]),
        pltpu.make_async_copy(um_hbm, um, sem_in.at[4]),
        pltpu.make_async_copy(d_hbm.at[2], d.at[2], sem_in.at[5]),
        pltpu.make_async_copy(dm_hbm, dm, sem_in.at[6]),
        pltpu.make_async_copy(ig_hbm, ig, sem_in.at[7]),
        pltpu.make_async_copy(og_hbm, og, sem_in.at[8]),
        pltpu.make_async_copy(d_hbm.at[0], d.at[0], sem_in.at[9]),
    ]
    for load in loads:
        load.start()
    for load in loads[:3]:
        load.wait()
    ig_store = pltpu.make_async_copy(ig, ig_out_hbm, sem_out.at[2 + FF // 256])
    stores = [
        pltpu.make_async_copy(cols_out.at[0], gate_hbm, sem_out.at[0]),
        pltpu.make_async_copy(cols_out.at[1], up_hbm, sem_out.at[1]),
    ]
    for which, mask in ((1, gm), (2, um)):
        if which == 2:
            loads[4].wait()
            loads[5].wait()
        for j in range(FF // 256):
            if which == 1 and j == 3:
                loads[3].wait()
            value = product(xt[...], d[which, :, j * 256 : (j + 1) * 256])
            for k in range(2):
                cols = pl.ds(j * 256 + k * BLOCK, BLOCK)
                for i in range(DIM // BLOCK):
                    rows = slice(i * BLOCK, (i + 1) * BLOCK)
                    keep = mask[i, 2 * j + k].astype(F32)
                    part = value[rows, k * BLOCK : (k + 1) * BLOCK] * keep
                    cols_out[which - 1, rows, cols] = part.astype(BF16)

        stores[which - 1].start()
    for load in loads[6:]:
        load.wait()
    ig_store.start()

    def store_rows(j):
        rows = pl.ds(j * 256, 256)
        return pltpu.make_async_copy(rows_out.at[rows], down_hbm.at[rows], sem_out.at[2 + j])

    for j in range(FF // 256):
        value = t_product(d[0, :, j * 256 : (j + 1) * 256], og[...])
        for k in range(2):
            rows = pl.ds(j * 256 + k * BLOCK, BLOCK)
            for i in range(DIM // BLOCK):
                cols = slice(i * BLOCK, (i + 1) * BLOCK)
                keep = dm[i, 2 * j + k].astype(F32)
                part = value[k * BLOCK : (k + 1) * BLOCK, cols] * keep
                rows_out[rows, cols] = part.astype(BF16)
        store_rows(j).start()

    ig_store.wait()
    for store in stores:
        store.wait()
    for j in range(FF // 256):
        store_rows(j).wait()


def grads(turned, out_grad, deltas, gate_mask, up_mask, down_mask, ig):
    any_spec = pl.BlockSpec(memory_space=pl.ANY)
    small = pltpu.SMEM((DIM // BLOCK, FF // BLOCK), jnp.int32)
    return pl.pallas_call(
        grads_kernel,
        out_shape=(
            jax.ShapeDtypeStruct((DIM, FF), BF16),
            jax.ShapeDtypeStruct((DIM, FF), BF16),
            jax.ShapeDtypeStruct((FF, DIM), BF16),
            jax.ShapeDtypeStruct((32, DIM), BF16),
        ),
        in_specs=[any_spec] * 7,
        out_specs=(any_spec,) * 4,
        scratch_shapes=[
            small,
            small,
            small,
            pltpu.VMEM((32, DIM), BF16),
            pltpu.VMEM((DIM, TOK), BF16),
            pltpu.VMEM((TOK, DIM), BF16),
            pltpu.VMEM((3, TOK, FF), BF16),
            pltpu.VMEM((2, DIM, FF), BF16),
            pltpu.VMEM((FF, DIM), BF16),
            pltpu.SemaphoreType.DMA((10,)),
            pltpu.SemaphoreType.DMA((3 + FF // 256,)),
        ],
        compiler_params=pltpu.CompilerParams(vmem_limit_bytes=62 * 2**20),
        name="grads",
    )(turned, out_grad, deltas, gate_mask, up_mask, down_mask.T, ig)


def shards(inputs, out_grad, gate_weight, up_weight, down_weight, gate_mask, up_mask, down_mask):
    deltas, turned, ig = exchange(inputs, out_grad, gate_weight, up_weight, down_weight, gate_mask, up_mask, down_mask)
    deltas = deltas.reshape(3, TOK, FF)
    gate_grad, up_grad, down_grad, input_grad = grads(turned, out_grad, deltas, gate_mask, up_mask, down_mask, ig)
    return (input_grad, gate_grad, up_grad, down_grad)


def solution(mesh):
    placed = (
        P(None, "row"),
        P(None, "row"),
        P("row", "col"),
        P("row", "col"),
        P("col", "row"),
        P("row", "col"),
        P("row", "col"),
        P("col", "row"),
    )
    return jax.shard_map(
        shards,
        mesh=mesh,
        in_specs=placed,
        out_specs=(P("col", "row"), P("row", "col"), P("row", "col"), P("col", "row")),
        check_vma=False,
    )
```

```python
import jax
import jax.numpy as jnp
from jax import lax
from jax.experimental import pallas as pl
from jax.experimental.pallas import tpu as pltpu
from jax.sharding import PartitionSpec as P

MESH = pl.DeviceIdType.MESH
F32 = jnp.float32
BF16 = jnp.bfloat16
BLOCK = 128
TOK = 512
DIM = 512
FF = 1792
HALF = FF // 2
CHUNKS = 4
ROWS = 64 // CHUNKS
GROUP = 2 * ROWS
SPAN = 4 * GROUP
PARTS = 1
STEPS = 3 * CHUNKS

LAG_RING = 1
LAG_FORWARD = 3
LAG_OWN = 5
LAG_FINAL = 8
LAG_RELAY = 10
LAG_CORE = 12
LAG_GRAD = 13
LAG_COL = 15
TURN = 13

R1, R2, R3, L1, L2, L3 = range(6)


def product(left, right):
    return jnp.dot(left, right, preferred_element_type=F32)


def product_t(left, right):
    return lax.dot_general(left, right, (((1,), (1,)), ((), ())), preferred_element_type=F32)


def t_product(left, right):
    return lax.dot_general(left, right, (((0,), (0,)), ((), ())), preferred_element_type=F32)


def exchange_kernel(
    x_hbm, og_hbm, wg_hbm, wu_hbm, wd_hbm, gm_hbm, um_hbm, dm_hbm,
    h_hbm, gate_hbm, up_hbm, xt_hbm, ig_out,
    gm, um, dm, x_own, og_own, xt, w_own, wd_own, core_out, core_in,
    part, send, ring, z_out, z_in, sums, deltas,
    ig, ig_x, ig_z, ig_sum, ig_in,
    local_sem, mask_sem, out_sem, core_s, core_r, ring_s, ring_r, z_s, z_r, ag_s, ag_r, x_s, x_r, zl_s, zl_r,
):
    row = lax.axis_index("row")
    col = lax.axis_index("col")
    y = row // 4
    h = (row // 2) % 2
    c = row % 2
    x = col // 4
    zl = col % 4
    up = lax.rem(y + 1, 4)
    down = lax.rem(y + 3, 4)
    far = lax.rem(y + 2, 4)

    def ring_dev(yy):
        return (yy * 4 + h * 2 + c, col)

    right = ring_dev(up)
    left = ring_dev(down)
    z_dev = (y * 4 + (1 - h) * 2 + c, col)
    core_dev = (y * 4 + h * 2 + (1 - c), col)
    own_cols = pl.ds(pl.multiple_of(c * HALF, 128), HALF)
    oth_cols = pl.ds(pl.multiple_of((1 - c) * HALF, 128), HALF)

    def x_dev(d):
        return (row, lax.rem(x + d, 4) * 4 + zl)

    def remote(src, dst, ss, rs, dev):
        return pltpu.make_async_remote_copy(
            src_ref=src, dst_ref=dst, send_sem=ss, recv_sem=rs, device_id=dev, device_id_type=MESH
        )

    def chunk(k):
        return lax.rem(k + CHUNKS // 2, CHUNKS)

    def owner(k):
        return chunk(k) // (CHUNKS // 4)

    def piece(yy, hh):
        return pl.ds(pl.multiple_of(yy * GROUP + hh * ROWS, ROWS), ROWS)

    def half(hh):
        return pl.ds(pl.multiple_of(hh * ROWS, ROWS), ROWS)

    loads = [
        pltpu.make_async_copy(x_hbm, x_own, local_sem.at[0]),
        pltpu.make_async_copy(wg_hbm.at[:, oth_cols], w_own.at[0, :, oth_cols], local_sem.at[1]),
        pltpu.make_async_copy(wg_hbm.at[:, own_cols], w_own.at[0, :, own_cols], local_sem.at[5]),
        pltpu.make_async_copy(wu_hbm, w_own.at[1], local_sem.at[2]),
        pltpu.make_async_copy(og_hbm, og_own, local_sem.at[3]),
        pltpu.make_async_copy(wd_hbm, wd_own, local_sem.at[4]),
    ]
    masks = [
        pltpu.make_async_copy(gm_hbm, gm, mask_sem.at[0]),
        pltpu.make_async_copy(um_hbm, um, mask_sem.at[1]),
        pltpu.make_async_copy(dm_hbm, dm, mask_sem.at[2]),
    ]
    for load in loads[:2] + masks + loads[2:]:
        load.start()

    bar = pltpu.get_barrier_semaphore()
    friends = [right, left, z_dev, core_dev] + [x_dev(d) for d in (1, 2, 3)]
    friends += [(row, x * 4 + lax.rem(zl + d, 4)) for d in (1, 2, 3)]
    for dev in friends:
        pl.semaphore_signal(bar, inc=1, device_id=dev, device_id_type=MESH)
    pl.semaphore_wait(bar, len(friends))

    def mask_cols(which, mask_ref, first, count):
        @pl.loop(0, count * HALF // BLOCK)
        def _(n):
            j = first * (HALF // BLOCK) + n
            cols = pl.ds(pl.multiple_of(j * BLOCK, BLOCK), BLOCK)
            for i in range(DIM // BLOCK):
                rows = pl.ds(i * BLOCK, BLOCK)
                keep = jnp.full((BLOCK, BLOCK), mask_ref[i, j].astype(F32), F32).astype(BF16)
                w_own[which, rows, cols] = w_own[which, rows, cols] * keep

    def mask_rows():
        @pl.loop(0, FF // BLOCK)
        def _(j):
            rows = pl.ds(pl.multiple_of(j * BLOCK, BLOCK), BLOCK)
            for i in range(DIM // BLOCK):
                cols = pl.ds(i * BLOCK, BLOCK)
                keep = jnp.full((BLOCK, BLOCK), dm[i, j].astype(F32), F32).astype(BF16)
                wd_own[rows, cols] = wd_own[rows, cols] * keep

    def core_copy(s):
        return remote(core_out.at[s], core_in.at[s], core_s.at[s], core_r.at[s], core_dev)

    def ring_copy(kind, s, yy, hh):
        dev = right if kind in (R1, R2, R3) else left
        return remote(send.at[s, piece(yy, hh)], ring.at[kind, s], ring_s.at[kind, s], ring_r.at[kind, s], dev)

    def ring_early(s):
        return [ring_copy(R1, s, far, 0), ring_copy(L1, s, far, 1), ring_copy(R2, s, up, 1), ring_copy(L2, s, down, 0)]

    def ring_late(s):
        return [ring_copy(R3, s, up, 0), ring_copy(L3, s, down, 1)]

    def z_copy(s):
        return remote(z_out.at[s], z_in.at[s], z_s.at[s], z_r.at[s], z_dev)

    def y_copy(m, k):
        def copy(i, yy, hh, dev):
            ref = deltas.at[m, k, yy, half(hh), own_cols]
            return remote(ref, ref, ag_s.at[m, k, i], ag_r.at[m, k, i], dev)

        return copy

    def pair_copy(m, k, cols):
        ref = deltas.at[m, k, :, :, cols]
        return remote(ref, ref, ag_s.at[m, k, 6], ag_r.at[m, k, 6], core_dev)

    def gather_own(*copies):
        for copy in copies:
            copy(0, y, 0, right).start()
            copy(3, y, 1, left).start()
        for copy in copies:
            copy(1, y, 1, right).start()
            copy(2, y, 0, left).start()

    def gather_relay(copy):
        copy(0, down, 0, right).wait_recv()
        copy(4, down, 0, right).start()
        copy(3, up, 1, left).wait_recv()
        copy(5, up, 1, left).start()

    def gather_rest(copy):
        copy(1, down, 1, right).wait_recv()
        copy(2, up, 0, left).wait_recv()
        copy(4, far, 0, right).wait_recv()
        copy(5, far, 1, left).wait_recv()

    def gather_drain(copy):
        for hh in range(2):
            copy(hh, y, hh, right).wait_send()
            copy(2 + hh, y, hh, left).wait_send()
        copy(4, down, 0, right).wait_send()
        copy(5, up, 1, left).wait_send()

    def out_copy(m, k):
        out = (h_hbm, gate_hbm, up_hbm)[m]
        return pltpu.make_async_copy(deltas.at[m, k], out.at[:, chunk(k)], out_sem.at[m, k])

    xt_copy = pltpu.make_async_copy(xt, xt_hbm, local_sem.at[6])

    def span(part):
        return pl.ds(part * (DIM // PARTS), DIM // PARTS)

    def x_copy(k, d, part):
        return remote(
            ig.at[k, lax.rem(x + d, 4), :, span(part)],
            ig_x.at[k, d - 1, :, span(part)],
            x_s.at[k, d - 1, part],
            x_r.at[k, d - 1, part],
            x_dev(d),
        )

    def zl_copy(k, part):
        slot = lax.rem(zl - owner(k) + 7, 4)
        part_of = lax.rem(chunk(k), CHUNKS // 4)
        return remote(
            ig_z.at[k, :, span(part)],
            ig_in.at[part_of, slot, :, span(part)],
            zl_s.at[k, part],
            zl_r.at[part_of, slot, part],
            (row, x * 4 + owner(k)),
        )

    def reduce_col(k):
        for part in range(PARTS):
            total = ig[k, x, :, span(part)]
            for d in (1, 2, 3):
                x_copy(k, d, part).wait_recv()
                total = total + ig_x[k, d - 1, :, span(part)]

            @pl.when(zl == owner(k))
            def _():
                ig_sum[lax.rem(chunk(k), CHUNKS // 4), :, span(part)] = total

            @pl.when(zl != owner(k))
            def _():
                ig_z[k, :, span(part)] = total.astype(BF16)
                zl_copy(k, part).start()

    def drain(k):
        for m in range(3):
            gather_drain(y_copy(m, k))
            pair_copy(m, k, own_cols).wait_send()
        for part in range(PARTS):
            for d in (1, 2, 3):
                x_copy(k, d, part).wait_send()

        @pl.when(zl != owner(k))
        def _():
            for part in range(PARTS):
                zl_copy(k, part).wait_send()

        for m in range(3):
            out_copy(m, k).wait()

    def at_chunk(s, lag, fn, count=CHUNKS):
        @pl.when((s >= lag + 2) & (s < 3 * count + lag) & (lax.rem(s + 3 * 32 - lag, 3) == 2))
        def _():
            fn((s - lag) // 3)

    @pl.loop(0, STEPS + LAG_COL)
    def _(s):
        @pl.when(s < STEPS)
        def _():
            m = lax.rem(s, 3)
            t = chunk(s // 3)

            @pl.when(s == 0)
            def _():
                loads[0].wait()
                loads[1].wait()
                masks[0].wait()
                mask_cols(0, gm, 1 - c, 1)

            @pl.when(s == 1)
            def _():
                loads[3].wait()
                masks[1].wait()
                mask_cols(1, um, 0, 2)

            @pl.when(s == 2)
            def _():
                loads[4].wait()
                loads[5].wait()
                masks[2].wait()
                mask_rows()

            @pl.when(m < 2)
            def _():
                rows = x_own[:, t].reshape(SPAN, DIM)
                core_out[s] = product(rows, w_own[m, :, oth_cols])
                core_copy(s).start()

                @pl.when(s == 0)
                def _():
                    loads[2].wait()
                    mask_cols(0, gm, c, 1)

                part[s] = product(rows, w_own[m, :, own_cols])

            @pl.when(m == 2)
            def _():
                rows = og_own[:, t].reshape(SPAN, DIM)
                core_out[s] = product_t(rows, wd_own[oth_cols, :])
                core_copy(s).start()
                part[s] = product_t(rows, wd_own[own_cols, :])

        @pl.when((s >= LAG_RING) & (s < STEPS + LAG_RING))
        def _():
            n = s - LAG_RING
            core_copy(n).wait_recv()
            value = part[n] + core_in[n]
            part[n] = value
            send[n] = value.astype(BF16)
            for copy in ring_early(n):
                copy.start()

        @pl.when((s >= LAG_FORWARD) & (s < STEPS + LAG_FORWARD))
        def _():
            n = s - LAG_FORWARD
            first = ring_early(n)[:2]
            onward = ring_late(n)
            first[0].wait_recv()
            send[n, piece(up, 0)] = (part[n, piece(up, 0)] + ring[R1, n].astype(F32)).astype(BF16)
            onward[0].start()
            first[1].wait_recv()
            send[n, piece(down, 1)] = (part[n, piece(down, 1)] + ring[L1, n].astype(F32)).astype(BF16)
            onward[1].start()

        @pl.when((s >= LAG_OWN) & (s < STEPS + LAG_OWN))
        def _():
            n = s - LAG_OWN
            for copy in ring_early(n)[2:] + ring_late(n):
                copy.wait_recv()
            first = part[n, piece(y, 0)] + ring[R3, n].astype(F32) + ring[L2, n].astype(F32)
            second = part[n, piece(y, 1)] + ring[L3, n].astype(F32) + ring[R2, n].astype(F32)
            sums[n, 0:ROWS] = first
            sums[n, ROWS : 2 * ROWS] = second
            z_out[n, 0:ROWS] = first.astype(BF16)
            z_out[n, ROWS : 2 * ROWS] = second.astype(BF16)
            z_copy(n).start()

        @pl.when((s >= LAG_FINAL) & (s < STEPS + LAG_FINAL))
        def _():
            n = s - LAG_FINAL
            z_copy(n).wait_recv()
            sums[n] = sums[n] + z_in[n].astype(F32)
            core_copy(n).wait_send()
            for copy in ring_early(n) + ring_late(n):
                copy.wait_send()
            z_copy(n).wait_send()

        @pl.when(s == TURN)
        def _():
            xt[...] = x_own[...].reshape(TOK, DIM).T
            xt_copy.start()

        def pointwise(k):
            gate = sums[3 * k]
            upv = sums[3 * k + 1]
            back = sums[3 * k + 2]
            sig = jax.nn.sigmoid(gate)
            slope = sig * (1.0 + gate * (1.0 - sig))
            deltas[1, k, y, :, own_cols] = (back * upv * slope).astype(BF16)
            deltas[2, k, y, :, own_cols] = (back * gate * sig).astype(BF16)
            gather_own(y_copy(1, k), y_copy(2, k))
            deltas[0, k, y, :, own_cols] = (gate * sig * upv).astype(BF16)

        def relay(k):
            gather_relay(y_copy(1, k))
            gather_relay(y_copy(2, k))
            gather_own(y_copy(0, k))

        def hidden_half(k, cols, rows):
            return product_t(deltas[1, k, :, :, cols].reshape(SPAN, HALF), w_own[0, rows, cols]) + product_t(
                deltas[2, k, :, :, cols].reshape(SPAN, HALF), w_own[1, rows, cols]
            )

        def to_core(k):
            for m in (1, 2):
                gather_rest(y_copy(m, k))
                pair_copy(m, k, own_cols).start()
            ig[k] = hidden_half(k, own_cols, pl.ds(0, DIM)).reshape(4, GROUP, DIM)
            gather_relay(y_copy(0, k))

        def grad(k):
            pair_copy(1, k, oth_cols).wait_recv()
            pair_copy(2, k, oth_cols).wait_recv()
            for part in range(PARTS):
                value = hidden_half(k, oth_cols, span(part)).reshape(4, GROUP, DIM // PARTS)
                ig[k, :, :, span(part)] = ig[k, :, :, span(part)] + value
                for d in (2, 1, 3):
                    x_copy(k, d, part).start()
            out_copy(1, k).start()
            out_copy(2, k).start()
            gather_rest(y_copy(0, k))
            pair_copy(0, k, own_cols).start()

        def finish(k):
            pair_copy(0, k, oth_cols).wait_recv()
            out_copy(0, k).start()
            reduce_col(k)

            @pl.when(k > 0)
            def _():
                drain(k - 1)

        at_chunk(s, LAG_FINAL, pointwise)
        at_chunk(s, LAG_RELAY, relay)
        at_chunk(s, LAG_CORE, to_core)
        at_chunk(s, LAG_GRAD, grad)
        at_chunk(s, LAG_COL, finish)

    for part_of in range(CHUNKS // 4):
        for part in range(PARTS):
            total = ig_sum[part_of, :, span(part)]
            for i in range(3):
                remote(
                    ig_z.at[0, :, span(part)],
                    ig_in.at[part_of, i, :, span(part)],
                    zl_s.at[0, part],
                    zl_r.at[part_of, i, part],
                    core_dev,
                ).wait_recv()
                total = total + ig_in[part_of, i, :, span(part)].astype(F32)
            ig_out[pl.ds(part_of * GROUP, GROUP), span(part)] = total.astype(BF16)

    drain(CHUNKS - 1)
    xt_copy.wait()


def exchange(inputs, out_grad, gate_weight, up_weight, down_weight, gate_mask, up_mask, down_mask):
    any_spec = pl.BlockSpec(memory_space=pl.ANY)
    small = pltpu.SMEM((DIM // BLOCK, FF // BLOCK), jnp.int32)
    dma = pltpu.SemaphoreType.DMA
    return pl.pallas_call(
        exchange_kernel,
        out_shape=(
            jax.ShapeDtypeStruct((4, CHUNKS, GROUP, FF), BF16),
            jax.ShapeDtypeStruct((4, CHUNKS, GROUP, FF), BF16),
            jax.ShapeDtypeStruct((4, CHUNKS, GROUP, FF), BF16),
            jax.ShapeDtypeStruct((DIM, TOK), BF16),
            jax.ShapeDtypeStruct((32, DIM), BF16),
        ),
        in_specs=[any_spec] * 8,
        out_specs=(any_spec,) * 4 + (pl.BlockSpec(memory_space=pltpu.VMEM),),
        scratch_shapes=[
            small,
            small,
            small,
            pltpu.VMEM((4, CHUNKS, GROUP, DIM), BF16),
            pltpu.VMEM((4, CHUNKS, GROUP, DIM), BF16),
            pltpu.VMEM((DIM, TOK), BF16),
            pltpu.VMEM((2, DIM, FF), BF16),
            pltpu.VMEM((FF, DIM), BF16),
            pltpu.VMEM((STEPS, SPAN, HALF), F32),
            pltpu.VMEM((STEPS, SPAN, HALF), F32),
            pltpu.VMEM((STEPS, SPAN, HALF), F32),
            pltpu.VMEM((STEPS, SPAN, HALF), BF16),
            pltpu.VMEM((6, STEPS, ROWS, HALF), BF16),
            pltpu.VMEM((STEPS, 2 * ROWS, HALF), BF16),
            pltpu.VMEM((STEPS, 2 * ROWS, HALF), BF16),
            pltpu.VMEM((STEPS, 2 * ROWS, HALF), F32),
            pltpu.VMEM((3, CHUNKS, 4, GROUP, FF), BF16),
            pltpu.VMEM((CHUNKS, 4, GROUP, DIM), F32),
            pltpu.VMEM((CHUNKS, 3, GROUP, DIM), F32),
            pltpu.VMEM((CHUNKS, GROUP, DIM), BF16),
            pltpu.VMEM((CHUNKS // 4, GROUP, DIM), F32),
            pltpu.VMEM((CHUNKS // 4, 3, GROUP, DIM), BF16),
            dma((7,)),
            dma((3,)),
            dma((3, CHUNKS)),
            dma((STEPS,)),
            dma((STEPS,)),
            dma((6, STEPS)),
            dma((6, STEPS)),
            dma((STEPS,)),
            dma((STEPS,)),
            dma((3, CHUNKS, 7)),
            dma((3, CHUNKS, 7)),
            dma((CHUNKS, 3, PARTS)),
            dma((CHUNKS, 3, PARTS)),
            dma((CHUNKS, PARTS)),
            dma((CHUNKS // 4, 3, PARTS)),
        ],
        compiler_params=pltpu.CompilerParams(
            collective_id=0, has_side_effects=True, vmem_limit_bytes=46 * 2**20
        ),
        name="exchange",
    )(
        inputs.reshape(4, CHUNKS, GROUP, DIM),
        out_grad.reshape(4, CHUNKS, GROUP, DIM),
        gate_weight,
        up_weight,
        down_weight,
        gate_mask,
        up_mask,
        down_mask.T,
    )


def grads_kernel(
    xt, og_hbm, h_in, gate_in, up_in, gm_hbm, um_hbm, dm_hbm, ig_hbm,
    gate_hbm, up_hbm, down_hbm, ig_out_hbm,
    gm, um, dm, ig, og, cols_out, rows_out, sem_in, sem_out,
):
    loads = [
        pltpu.make_async_copy(gm_hbm, gm, sem_in.at[0]),
        pltpu.make_async_copy(um_hbm, um, sem_in.at[1]),
        pltpu.make_async_copy(dm_hbm, dm, sem_in.at[2]),
        pltpu.make_async_copy(ig_hbm, ig, sem_in.at[3]),
        pltpu.make_async_copy(og_hbm, og, sem_in.at[4]),
    ]
    for load in loads:
        load.start()
    loads[0].wait()
    ig_store = pltpu.make_async_copy(ig, ig_out_hbm, sem_out.at[2 + FF // 256])
    stores = [
        pltpu.make_async_copy(cols_out.at[0], gate_hbm, sem_out.at[0]),
        pltpu.make_async_copy(cols_out.at[1], up_hbm, sem_out.at[1]),
    ]
    for which, mask in ((1, gm), (2, um)):
        if which == 2:
            loads[1].wait()
        source = (gate_in, up_in)[which - 1]
        for j in range(FF // 256):
            value = product(xt[...], source[:, j * 256 : (j + 1) * 256])
            for k in range(2):
                cols = pl.ds(j * 256 + k * BLOCK, BLOCK)
                for i in range(DIM // BLOCK):
                    rows = slice(i * BLOCK, (i + 1) * BLOCK)
                    keep = mask[i, 2 * j + k].astype(F32)
                    part = value[rows, k * BLOCK : (k + 1) * BLOCK] * keep
                    cols_out[which - 1, rows, cols] = part.astype(BF16)

        stores[which - 1].start()
    for load in loads[2:]:
        load.wait()
    ig_store.start()

    def store_rows(j):
        rows = pl.ds(j * 256, 256)
        return pltpu.make_async_copy(rows_out.at[rows], down_hbm.at[rows], sem_out.at[2 + j])

    for j in range(FF // 256):
        value = t_product(h_in[:, j * 256 : (j + 1) * 256], og[...])
        for k in range(2):
            rows = pl.ds(j * 256 + k * BLOCK, BLOCK)
            for i in range(DIM // BLOCK):
                cols = slice(i * BLOCK, (i + 1) * BLOCK)
                keep = dm[i, 2 * j + k].astype(F32)
                part = value[k * BLOCK : (k + 1) * BLOCK, cols] * keep
                rows_out[rows, cols] = part.astype(BF16)
        store_rows(j).start()

    ig_store.wait()
    for store in stores:
        store.wait()
    for j in range(FF // 256):
        store_rows(j).wait()


def grads(turned, out_grad, hidden, gate, up, gate_mask, up_mask, down_mask, ig):
    any_spec = pl.BlockSpec(memory_space=pl.ANY)
    vmem = pl.BlockSpec(memory_space=pltpu.VMEM)
    small = pltpu.SMEM((DIM // BLOCK, FF // BLOCK), jnp.int32)
    return pl.pallas_call(
        grads_kernel,
        out_shape=(
            jax.ShapeDtypeStruct((DIM, FF), BF16),
            jax.ShapeDtypeStruct((DIM, FF), BF16),
            jax.ShapeDtypeStruct((FF, DIM), BF16),
            jax.ShapeDtypeStruct((32, DIM), BF16),
        ),
        in_specs=[vmem, any_spec, vmem, vmem, vmem] + [any_spec] * 4,
        out_specs=(any_spec,) * 4,
        scratch_shapes=[
            small,
            small,
            small,
            pltpu.VMEM((32, DIM), BF16),
            pltpu.VMEM((TOK, DIM), BF16),
            pltpu.VMEM((2, DIM, FF), BF16),
            pltpu.VMEM((FF, DIM), BF16),
            pltpu.SemaphoreType.DMA((5,)),
            pltpu.SemaphoreType.DMA((3 + FF // 256,)),
        ],
        compiler_params=pltpu.CompilerParams(vmem_limit_bytes=44 * 2**20),
        name="grads",
    )(turned, out_grad, hidden, gate, up, gate_mask, up_mask, down_mask.T, ig)


def shards(inputs, out_grad, gate_weight, up_weight, down_weight, gate_mask, up_mask, down_mask):
    hidden, gate, up, turned, ig = exchange(inputs, out_grad, gate_weight, up_weight, down_weight, gate_mask, up_mask, down_mask)
    hidden, gate, up = (value.reshape(TOK, FF) for value in (hidden, gate, up))
    gate_grad, up_grad, down_grad, input_grad = grads(turned, out_grad, hidden, gate, up, gate_mask, up_mask, down_mask, ig)
    return (input_grad, gate_grad, up_grad, down_grad)


def solution(mesh):
    placed = (
        P(None, "row"),
        P(None, "row"),
        P("row", "col"),
        P("row", "col"),
        P("col", "row"),
        P("row", "col"),
        P("row", "col"),
        P("col", "row"),
    )
    return jax.shard_map(
        shards,
        mesh=mesh,
        in_specs=placed,
        out_specs=(P("col", "row"), P("row", "col"), P("row", "col"), P("col", "row")),
        check_vma=False,
    )
```
